512 devices in a mesh: obs: 16 (over x, y), tm: 32 (over z, core).
Axes of the slice: x: 4, y: 4, z: 16, core: 2. Of those that a mesh axis runs over, the one named last changes fastest.
Arguments:
- flow: float32 [5, 2048, 8192], P(None, 'tm', 'obs'), may hold values from -6 to 6
- point_pos: float32 [3, 8192], P(None, 'obs'), may hold values from -1 to 1
- area_vec: float32 [3, 8192], P(None, 'obs'), may hold values from -3.1819806 to 3.1819806
- observer_angles: float32 [2, 2048], P(None, 'obs'), may hold values from -3.140625 to 3.140625
- band_offset: int32 [16, 16], replicated, may hold values from 0 to 61, as said below
Outputs:
- pressure: float32 [2048, 2048], P('tm', 'obs')
The draws below stay inside these ranges and needn't reach their ends.
Inputs may be any that keep to these rules, and one draw needn't show every extreme that they name: band_offset[g, b] is the whole number of time steps added to every delay from point block b to observer group g; both 0 and 61 occur.
All inputs are finite; a program needn't handle non-finite values.
Results may differ from the reference program's by a relative error of at most 0.0041.
Values may be sent and summed in bfloat16 or wider, within the bound.
No kernel may reach another device: no remote copies, remote signals or barrier semaphores. Data moves between devices by JAX's collectives and lax.ppermute only.
A program may use at most 64 MiB of HBM per device.

```python
import math
import jax
import jax.numpy as jnp
from jax import lax

PTS_DEV = 512
GROUP_OBS = 128
BLOCK = 64
LAGS = 4
GROUPS = 16
OBSERVERS = 2048
POINTS = 8192
STEPS = 2048
MAX_DELAY = 61


def draw_band_offset(key, part):
    entries = GROUPS * GROUPS
    key_values, key_first, key_second = jax.random.split(key, 3)
    values = jax.random.randint(key_values, (entries,), 0, MAX_DELAY + 1)
    first_slot = jax.random.randint(key_first, (), 0, entries)
    second_slot = (first_slot + 1 + jax.random.randint(key_second, (), 0, entries - 1)) % entries
    position = jnp.arange(entries)
    values = jnp.where(position == first_slot, MAX_DELAY, values)
    values = jnp.where(position == second_slot, 0, values)
    return values.reshape(GROUPS, GROUPS).astype(jnp.int32)


def block_scale(own_key, dims, shards, least, high):
    def one(dim, parts):
        heights = jax.random.uniform(jax.random.fold_in(jax.random.fold_in(own_key, 6), dim), (parts,), jnp.float32, least / len(shards), high / len(shards))
        return jnp.repeat(jnp.exp(heights), dims[dim] // parts).reshape((-1,) + (1,) * (len(dims) - dim - 1))

    gain = one(*shards[0])
    for cut in shards[1:]:
        gain = gain * one(*cut)
    return gain


def noise(key, extent, spread, most, pieces=(), kind=jnp.bfloat16):
    factor_of = block_scale(key, extent, pieces, -0.22, 0.18) if pieces else 1.0
    array = jax.random.normal(key, extent, jnp.float32) * spread * factor_of
    return jnp.minimum(jnp.maximum(array, -most), most).astype(kind)


def setup_inputs(seed: int = 0) -> dict:
    key_list = jax.random.split(jax.random.key(seed), 6)
    flow = noise(key_list[0], (5, STEPS, POINTS), 1.0, 6.0, ((1, 32), (2, 16)), jnp.float32)
    point_pos = jnp.clip(jax.random.uniform(key_list[1], (3, POINTS), jnp.float32, -1.0, 1.0) * block_scale(key_list[1], (3, POINTS), ((1, 16),), -0.4, 0.0), -1.0, 1.0)
    area_vec = noise(key_list[2], (3, POINTS), (48.0 / POINTS ** 0.5), 3.1819806, ((1, 16),), jnp.float32)
    observer_angles = jnp.clip(jax.random.uniform(key_list[3], (2, OBSERVERS), jnp.float32, -3.140625, 3.140625), -3.140625, 3.140625)
    band_offset = draw_band_offset(jax.random.fold_in(key_list[5], 71), 0)
    return dict(flow=flow, point_pos=point_pos, area_vec=area_vec, observer_angles=observer_angles, band_offset=band_offset)


FOUR_PI_INV = 1.0 / (4.0 * math.pi)
NEAR_RANGE = 3.25
SOUND_STEP = 1.17
SPHERE_RADIUS = 5.0

def observer_xyz(angles):
    azimuth = angles[0]
    elevation = angles[1]
    return SPHERE_RADIUS * jnp.stack([jnp.cos(azimuth) * jnp.cos(elevation), jnp.sin(azimuth) * jnp.cos(elevation), jnp.sin(elevation)])

def source_terms(rimmed, area_vec):
    density = 1.0 + 0.2 * rimmed[0]
    velocity = 0.4 * rimmed[1:4]
    pressure = rimmed[4]
    normal_flux = lax.optimization_barrier(jnp.sum(velocity * area_vec[:, None, :], axis=0))
    mass_flux = density * normal_flux
    loading = pressure[None] * area_vec[:, None, :] + density[None] * velocity * normal_flux[None]
    stacked = jnp.concatenate([mass_flux[None], loading], axis=0)
    rate_terms = 0.5 * (stacked[:, 2:] - stacked[:, :-2])
    return jnp.concatenate([rate_terms, loading[:, 1:-1]], axis=0).astype(jnp.bfloat16)

def pair_weights(observers, points, lag_count):
    separation = observers[:, None, :] - points[:, :, None]
    distance = jnp.sqrt(lax.optimization_barrier(jnp.sum(separation * separation, axis=0)))
    inverse = 1.0 / distance
    direction = separation * inverse[None]
    lag_steps = (distance - NEAR_RANGE) / SOUND_STEP
    shifts = jnp.arange(lag_count).astype(distance.dtype)
    tent_weights = jnp.maximum(0.0, 1.0 - jnp.abs(shifts[None, :, None] - lag_steps[:, None, :]))
    coeffs = jnp.concatenate([inverse[None], direction * (inverse / SOUND_STEP)[None], direction * (inverse * inverse)[None]], axis=0) * FOUR_PI_INV
    return (coeffs[:, :, None, :] * tent_weights[None]).astype(jnp.bfloat16)

def placed_whole(shard_terms, weights, offset, buffer_len):
    product = jnp.einsum('kts,kswo->two', shard_terms.astype(jnp.float32), weights.astype(jnp.float32))
    lag_count = product.shape[1]
    combined = jnp.pad(product[:, 0], ((0, lag_count - 1), (0, 0)))
    for lag_index in range(1, lag_count):
        combined = combined + jnp.pad(product[:, lag_index], ((lag_index, lag_count - 1 - lag_index), (0, 0)))
    canvas = jnp.zeros((buffer_len, product.shape[2]), jnp.float32)
    return lax.dynamic_update_slice(canvas, combined, (offset.astype(jnp.int32), jnp.zeros((), jnp.int32)))

def reference(flow, point_pos, area_vec, observer_angles, band_offset):
    padded = jnp.pad(flow, ((0, 0), (1, 1), (0, 0)))
    all_terms = source_terms(padded, area_vec)
    places = observer_xyz(observer_angles)

    def one_group(group_index):
        group_places = lax.dynamic_slice_in_dim(places, group_index * GROUP_OBS, GROUP_OBS, 1)

        def one_block(accumulated, block_index):
            shard_points = lax.dynamic_slice_in_dim(point_pos, block_index * PTS_DEV, PTS_DEV, 1)
            shard_terms = lax.dynamic_slice_in_dim(all_terms, block_index * PTS_DEV, PTS_DEV, 2)
            weights = pair_weights(group_places, shard_points, LAGS)
            return (accumulated + placed_whole(shard_terms, weights, band_offset[group_index, block_index], STEPS + BLOCK), None)
        initial = jnp.zeros((STEPS + BLOCK, GROUP_OBS), jnp.float32)
        accumulated, unused = lax.scan(one_block, initial, jnp.arange(GROUPS, dtype=jnp.int32))
        return accumulated[:STEPS]
    per_group = lax.map(one_group, jnp.arange(GROUPS, dtype=jnp.int32))
    return jnp.transpose(per_group, (1, 0, 2)).reshape(STEPS, OBSERVERS)
```

```python
import math

import jax
import jax.numpy as jnp
from jax import lax
from jax.experimental import pallas as pl
from jax.experimental.pallas import tpu as pltpu
from jax.sharding import PartitionSpec as P

LAGS = 4
FOUR_PI_INV = 1.0 / (4.0 * math.pi)
NEAR_RANGE = 3.25
SOUND_STEP = 1.17
SPHERE_RADIUS = 5.0
COMPS = 4
BACK = 8
CHUNK = 16


def terms_kernel(edge_ref, flow_ref, low_ref, high_ref, area_ref, point_ref, terms_ref, spread_ref, rows_ref):
    steps = flow_ref.shape[1]
    rows_ref[:, :BACK, :] = jnp.zeros_like(rows_ref[:, :BACK, :])
    rows_ref[:, BACK + steps :, :] = jnp.zeros_like(rows_ref[:, BACK + steps :, :])
    rows_ref[:, BACK - LAGS : BACK, :] = low_ref[...]
    rows_ref[:, BACK : BACK + steps, :] = flow_ref[...]
    rows_ref[:, BACK + steps : BACK + steps + 1, :] = high_ref[...]
    area = [area_ref[i : i + 1, :] for i in range(3)]
    point = [point_ref[i : i + 1, :] for i in range(3)]
    density = 1.0 + 0.2 * rows_ref[0]
    velocity = [0.4 * rows_ref[1 + i] for i in range(3)]
    pressure = rows_ref[4]
    normal_flux = velocity[0] * area[0] + velocity[1] * area[1] + velocity[2] * area[2]
    mass_flux = density * normal_flux
    loading = [pressure * area[i] + mass_flux * velocity[i] for i in range(3)]
    reach = SPHERE_RADIUS**2 + point[0] * point[0] + point[1] * point[1] + point[2] * point[2]
    first = BACK - LAGS + 1
    count = steps + LAGS - 1
    row = lax.broadcasted_iota(jnp.int32, (count, area_ref.shape[1]), 0)
    keep = jnp.logical_or(row >= LAGS - 1, edge_ref[0] != 0)

    def rate(x):
        return 0.5 * (x[first + 1 : first + 1 + count] - x[first - 1 : first - 1 + count])

    mass_rate = rate(mass_flux)
    load_rate = [rate(x) for x in loading]
    load = [x[first : first + count] for x in loading]
    along_rate = point[0] * load_rate[0] + point[1] * load_rate[1] + point[2] * load_rate[2]
    along = point[0] * load[0] + point[1] * load[1] + point[2] * load[2]
    far = load_rate + [-along_rate]
    near = [load[i] - (2.0 * point[i]) * mass_rate for i in range(3)] + [reach * mass_rate - along]
    width = area_ref.shape[1]
    for family, parts in enumerate((far, near)):
        for comp, part in enumerate(parts):
            part = jnp.where(keep, part, 0.0)
            for lag in range(LAGS):
                start = LAGS - 1 - lag
                terms_ref[comp * steps : (comp + 1) * steps, pl.ds((family * LAGS + lag) * width, width)] = part[
                    start : start + steps
                ].astype(jnp.bfloat16)
    turned = jnp.transpose(jnp.concatenate([point_ref[...], jnp.zeros((5, width), jnp.float32)], axis=0))
    for i in range(3):
        spread_ref[i] = jnp.broadcast_to(turned[:, i : i + 1], spread_ref.shape[1:])


def fill_weights(places, spread_ref, weights_ref):
    width = spread_ref.shape[1]
    lanes = places[0].shape[1] // spread_ref.shape[2]
    for start in range(0, width, CHUNK):
        sep = [
            places[i] - jnp.concatenate([spread_ref[i, start : start + CHUNK, :]] * lanes, axis=1) for i in range(3)
        ]
        square = sep[0] * sep[0] + sep[1] * sep[1] + sep[2] * sep[2]
        inverse = lax.rsqrt(square)
        lag = (square * inverse) * (1.0 / SOUND_STEP) - (NEAR_RANGE / SOUND_STEP)
        behind = 1.0 - lag
        beyond = lag - 2.0
        tents = (
            jnp.maximum(behind, 0.0),
            jnp.maximum(jnp.minimum(lag, 2.0 - lag), 0.0),
            jnp.maximum(jnp.minimum(lag - 1.0, 3.0 - lag), 0.0),
            jnp.maximum(beyond, 0.0),
        )
        inverse_square = inverse * inverse
        far = inverse_square * (FOUR_PI_INV / SOUND_STEP)
        near = (inverse_square * inverse) * FOUR_PI_INV
        for family, coeff in enumerate((far, near)):
            for index, tent in enumerate(tents):
                base = (family * LAGS + index) * width + start
                weights_ref[base : base + CHUNK, :] = (coeff * tent).astype(jnp.bfloat16)


def pair_kernel(angle_ref, terms_ref, spread_ref, sums_ref, places_ref, weights_ref):
    step = pl.program_id(0)

    @pl.when(step == 0)
    def _():
        azimuth = angle_ref[:, 0, :]
        elevation = angle_ref[:, 1, :]
        flat = SPHERE_RADIUS * jnp.cos(elevation)
        places_ref[0] = flat * jnp.cos(azimuth)
        places_ref[1] = flat * jnp.sin(azimuth)
        places_ref[2] = SPHERE_RADIUS * jnp.sin(elevation)

    pair = sums_ref.shape[0]
    places = [
        jnp.concatenate([places_ref[i, pl.ds(step * pair + j, 1), :] for j in range(pair)], axis=1) for i in range(3)
    ]
    fill_weights(places, spread_ref, weights_ref)
    product = jnp.dot(terms_ref[...], weights_ref[...], preferred_element_type=jnp.float32)
    steps = sums_ref.shape[1]
    lanes = sums_ref.shape[2]
    total = product[3 * steps :]
    for i in range(3):
        total = total + places[i] * product[i * steps : (i + 1) * steps]
    for j in range(pair):
        sums_ref[j] = total[:, j * lanes : (j + 1) * lanes]


def place_kernel(offset_ref, sums_ref, out_ref, later_ref, canvas_ref):
    groups, steps, lanes = sums_ref.shape
    canvas_ref[...] = jnp.zeros_like(canvas_ref)
    for block in range(groups):
        span = pl.ds(offset_ref[block], steps)
        canvas_ref[span, :] = canvas_ref[span, :] + sums_ref[block]
    out_ref[...] = canvas_ref[:steps]
    later_ref[...] = canvas_ref[steps : 2 * steps]


VMEM = pl.BlockSpec(memory_space=pltpu.VMEM)
SMEM = pl.BlockSpec(memory_space=pltpu.SMEM)


def local(flow, point_pos, area_vec, observer_angles, band_offset):
    steps = flow.shape[1]
    width = flow.shape[2]
    groups = lax.axis_size("obs")
    lanes = observer_angles.shape[1]
    times = lax.axis_size("tm")
    angles = lax.all_to_all(
        jnp.broadcast_to(observer_angles[None], (groups, 2, lanes)), "obs", 0, 0, tiled=True
    )
    low = lax.ppermute(flow[:, steps - LAGS :], "tm", [(i, i + 1) for i in range(times - 1)])
    high = lax.ppermute(flow[:, :1], "tm", [(i + 1, i) for i in range(times - 1)])
    edge = lax.axis_index("tm").astype(jnp.int32).reshape(1)
    depth = 2 * LAGS * width
    terms, spread = pl.pallas_call(
        terms_kernel,
        out_shape=(
            jax.ShapeDtypeStruct((COMPS * steps, depth), jnp.bfloat16),
            jax.ShapeDtypeStruct((3, width, lanes), jnp.float32),
        ),
        in_specs=[SMEM] + [VMEM] * 5,
        out_specs=(VMEM, VMEM),
        scratch_shapes=[pltpu.VMEM((5, steps + 2 * BACK, width), jnp.float32)],
        name="terms",
    )(edge, flow, low, high, area_vec, point_pos)
    pair = 2
    sums = pl.pallas_call(
        pair_kernel,
        grid=(groups // pair,),
        out_shape=jax.ShapeDtypeStruct((groups, steps, lanes), jnp.float32),
        in_specs=[VMEM] * 3,
        out_specs=pl.BlockSpec((pair, steps, lanes), lambda i: (i, 0, 0)),
        scratch_shapes=[
            pltpu.VMEM((3, groups, lanes), jnp.float32),
            pltpu.VMEM((depth, pair * lanes), jnp.bfloat16),
        ],
        name="pairs",
    )(angles, terms, spread)
    sums = lax.all_to_all(sums, "obs", 0, 0, tiled=True)
    offsets = lax.dynamic_index_in_dim(band_offset, lax.axis_index("obs"), 0, keepdims=False)
    out, later = pl.pallas_call(
        place_kernel,
        out_shape=(jax.ShapeDtypeStruct((steps, lanes), jnp.float32),) * 2,
        in_specs=[SMEM, VMEM],
        out_specs=(VMEM, VMEM),
        scratch_shapes=[pltpu.VMEM((2 * steps, lanes), jnp.float32)],
        name="place",
    )(offsets, sums)
    carried = lax.ppermute(later, "tm", [(i, i + 1) for i in range(times - 1)])
    return out + carried


def solution(mesh):
    in_specs = (P(None, "tm", "obs"), P(None, "obs"), P(None, "obs"), P(None, "obs"), P())
    out_specs = P("tm", "obs")
    return jax.shard_map(local, mesh=mesh, in_specs=in_specs, out_specs=out_specs, check_vma=False)
```

```python
import math

import jax
import jax.numpy as jnp
from jax import lax
from jax.experimental import pallas as pl
from jax.experimental.pallas import tpu as pltpu
from jax.sharding import PartitionSpec as P

LAGS = 4
NEAR_RANGE = 3.25
SOUND_STEP = 1.17
RADIUS = 5.0 / SOUND_STEP
NEAREST = NEAR_RANGE / SOUND_STEP
SCALE = 1.0 / (4.0 * math.pi * SOUND_STEP * SOUND_STEP)
COMPS = 4
ROWS = 8
LANES = 128
CHUNK = 16
PARTS = 8
LEAD = 0


def prep_kernel(flow_ref, angle_ref, wide_ref, low_ref, high_ref, edges_ref, sem):
    steps = flow_ref.shape[1]
    copies = [
        pltpu.make_async_copy(flow_ref.at[:, pl.ds(start, ROWS), :], edges_ref.at[side], sem.at[side])
        for side, start in enumerate((steps - ROWS, 0))
    ]
    for copy in copies:
        copy.start()
    for group in range(wide_ref.shape[0]):
        wide_ref[group] = angle_ref[...]
    for copy in copies:
        copy.wait()
    low_ref[...] = edges_ref[0, :, ROWS - LAGS :, :]
    high_ref[...] = edges_ref[1, :, :1, :]


def terms_kernel(edge_ref, flow_ref, low_ref, high_ref, area_ref, point_ref, terms_ref, spread_ref, field_ref, part_ref):
    steps = flow_ref.shape[1]
    width = flow_ref.shape[2]
    count = steps + ROWS
    for cut in range(width // LANES):
        lanes = slice(cut * LANES, (cut + 1) * LANES)
        area = [SCALE * area_ref[i : i + 1, lanes] for i in range(3)]
        point = [(1.0 / SOUND_STEP) * point_ref[i : i + 1, lanes] for i in range(3)]

        def fields(source, start, rows):
            density = 1.0 + 0.2 * source[0, :, lanes]
            velocity = [0.4 * source[1 + i, :, lanes] for i in range(3)]
            pressure = source[4, :, lanes]
            normal_flux = velocity[0] * area[0] + velocity[1] * area[1] + velocity[2] * area[2]
            mass_flux = density * normal_flux
            field_ref[0, cut, start : start + rows, :] = mass_flux
            for i in range(3):
                field_ref[1 + i, cut, start : start + rows, :] = pressure * area[i] + mass_flux * velocity[i]

        field_ref[:, cut, ROWS + steps :, :] = jnp.zeros((4, ROWS, LANES), jnp.float32)
        fields(low_ref, ROWS - LAGS, LAGS)
        fields(flow_ref, ROWS, steps)
        fields(high_ref, ROWS + steps, 1)
        first = ROWS - LAGS + 1
        row = lax.broadcasted_iota(jnp.int32, (count, LANES), 0)
        keep = jnp.where(jnp.logical_or(row >= LAGS - 1, edge_ref[0] != 0), 1.0, 0.0)
        rates = [
            (0.5 * keep)
            * (field_ref[k, cut, first + 1 : first + 1 + count, :] - field_ref[k, cut, first - 1 : first - 1 + count, :])
            for k in range(4)
        ]
        loads = [keep * field_ref[1 + i, cut, first : first + count, :] for i in range(3)]
        reach = RADIUS * RADIUS + point[0] * point[0] + point[1] * point[1] + point[2] * point[2]
        mass_rate = SOUND_STEP * rates[0]
        far = rates[1:] + [-(point[0] * rates[1] + point[1] * rates[2] + point[2] * rates[3])]
        near = [loads[i] - (2.0 * point[i]) * mass_rate for i in range(3)]
        near.append(reach * mass_rate - (point[0] * loads[0] + point[1] * loads[1] + point[2] * loads[2]))
        for family, parts in enumerate((far, near)):
            for comp, part in enumerate(parts):
                part_ref[cut, family * COMPS + comp] = part
        for family in range(2):
            for comp in range(COMPS):
                for lag in range(LAGS):
                    start = LAGS - 1 - lag
                    block = (cut * 2 + family) * LAGS + lag
                    terms_ref[block, comp * steps : (comp + 1) * steps, :] = part_ref[
                        cut, family * COMPS + comp, start : start + steps, :
                    ].astype(jnp.bfloat16)
        turned = jnp.transpose(
            jnp.concatenate([2.0 * point[0], 2.0 * point[1], 2.0 * point[2], reach] * 2, axis=0)
        )
        for i in range(4):
            spread_ref[i, lanes, :] = jnp.broadcast_to(turned[:, i : i + 1], (LANES, LANES))


def fill_weights(places, spread_ref, weights_ref, half, part):
    span = spread_ref.shape[1] // 2
    for start in range(span * part // PARTS, span * (part + 1) // PARTS, CHUNK):
        rows = slice(half * span + start, half * span + start + CHUNK)
        spread = [spread_ref[i, rows, :] for i in range(4)]
        for group, place in enumerate(places):
            square = spread[3] - place[0] * spread[0] - place[1] * spread[1] - place[2] * spread[2]
            inverse = lax.rsqrt(square)
            behind = (1.0 + NEAREST) - square * inverse
            first = jnp.maximum(behind, 0.0)
            passed = first - behind
            last = jnp.maximum(passed - 1.0, 0.0)
            middle = jnp.minimum(passed, 1.0)
            tents = (first, (1.0 - middle) - first, middle - last, last)
            far = inverse * inverse
            near = far * inverse
            quarter = start // LANES
            for family, coeff in enumerate((far, near)):
                for index, tent in enumerate(tents):
                    base = ((quarter * 2 + family) * LAGS + index) * LANES + start % LANES
                    weights_ref[group, base : base + CHUNK, :] = (coeff * tent).astype(jnp.bfloat16)


def sine_cosine(angle):
    half = 0.5 * angle
    square = half * half
    sine = cosine = 0.0
    for k in range(7, -1, -1):
        cosine = cosine * square + (-1.0) ** k / math.factorial(2 * k)
        sine = sine * square + (-1.0) ** k / math.factorial(2 * k + 1)
    sine = half * sine
    return 2.0 * sine * cosine, 1.0 - 2.0 * sine * sine


def pair_kernel(angle_ref, terms_ref, spread_ref, sums_ref, angles_ref, places_ref, even_ref, odd_ref, held_ref):
    groups, steps, lanes = sums_ref.shape
    for group in range(groups):
        for i in range(2):
            angles_ref[i, group : group + 1, :] = angle_ref[group, i : i + 1, :]
    sine, cosine = sine_cosine(angles_ref[0])
    rise, flat = sine_cosine(angles_ref[1])
    places_ref[0] = RADIUS * (cosine * flat)
    places_ref[1] = RADIUS * (sine * flat)
    places_ref[2] = RADIUS * rise
    pair = even_ref.shape[0]
    turns = groups // pair
    blocks = terms_ref.shape[0] // 2

    def places_of(turn):
        return [[places_ref[i, pl.ds(turn * pair + j, 1), :] for i in range(3)] for j in range(pair)]

    def multiply(half, weights_ref, make):
        total = None
        for part in range(PARTS):
            span = range(blocks * part // PARTS, blocks * (part + 1) // PARTS)
            terms = jnp.concatenate([terms_ref[half * blocks + k] for k in span], axis=1)
            rows = slice(span[0] * LANES, (span[-1] + 1) * LANES)
            weights = jnp.concatenate([weights_ref[j, rows, :] for j in range(pair)], axis=1)
            piece = jnp.dot(terms, weights, preferred_element_type=jnp.float32)
            total = piece if total is None else total + piece
            if part >= LEAD:
                make(part - LEAD)
        return total

    def finish(turn, total):
        total = total + held_ref[...]
        for j, place in enumerate(places_of(turn)):
            mine = total[:, j * lanes : (j + 1) * lanes]
            result = mine[3 * steps :]
            for i in range(3):
                result = result + place[i] * mine[i * steps : (i + 1) * steps]
            sums_ref[turn * pair + j] = result

    for part in range(PARTS):
        fill_weights(places_of(0), spread_ref, even_ref, 0, part)

    def body(turn, carry):
        @pl.when(turn >= 0)
        def _():
            places = places_of(turn)

            def make(part):
                fill_weights(places, spread_ref, odd_ref, 1, part)

            held_ref[...] = multiply(0, even_ref, make)
            for part in range(PARTS - LEAD, PARTS):
                make(part)

        @pl.when(turn < turns - 1)
        def _():
            places = places_of(turn + 1)

            def make(part):
                fill_weights(places, spread_ref, even_ref, 0, part)

            finish(turn, multiply(1, odd_ref, make))
            for part in range(PARTS - LEAD, PARTS):
                make(part)

        return carry

    lax.fori_loop(0, turns, body, 0)
    finish(turns - 1, multiply(1, odd_ref, lambda part: None))


def place_kernel(offset_ref, sums_ref, out_ref, later_ref, canvas_ref):
    groups, steps, lanes = sums_ref.shape
    canvas_ref[...] = jnp.zeros_like(canvas_ref)
    for block in range(groups):
        span = pl.ds(offset_ref[block], steps)
        canvas_ref[span, :] = canvas_ref[span, :] + sums_ref[block]
    out_ref[...] = canvas_ref[:steps]
    later_ref[...] = canvas_ref[steps : 2 * steps]


VMEM = pl.BlockSpec(memory_space=pltpu.VMEM)
SMEM = pl.BlockSpec(memory_space=pltpu.SMEM)
HBM = pl.BlockSpec(memory_space=pltpu.HBM)


def near_core(array):
    return pltpu.with_memory_space_constraint(array, pltpu.VMEM)


def local(flow, point_pos, area_vec, observer_angles, band_offset):
    steps = flow.shape[1]
    width = flow.shape[2]
    groups = lax.axis_size("obs")
    lanes = observer_angles.shape[1]
    times = lax.axis_size("tm")
    wide, low, high = pl.pallas_call(
        prep_kernel,
        out_shape=(
            pltpu.VMEM((groups, 2, lanes), jnp.float32),
            pltpu.VMEM((5, LAGS, width), jnp.float32),
            pltpu.VMEM((5, 1, width), jnp.float32),
        ),
        in_specs=[HBM, VMEM],
        out_specs=(VMEM,) * 3,
        scratch_shapes=[pltpu.VMEM((2, 5, ROWS, width), jnp.float32), pltpu.SemaphoreType.DMA((2,))],
        compiler_params=pltpu.CompilerParams(vmem_limit_bytes=8 << 20),
        name="prep",
    )(flow, observer_angles)
    angles = lax.all_to_all(wide, "obs", 0, 0, tiled=True)
    low = lax.ppermute(low, "tm", [(i, i + 1) for i in range(times - 1)])
    high = lax.ppermute(high, "tm", [(i + 1, i) for i in range(times - 1)])
    edge = lax.axis_index("tm").astype(jnp.int32).reshape(1)
    depth = 2 * LAGS * width
    terms, spread = pl.pallas_call(
        terms_kernel,
        out_shape=(
            pltpu.VMEM((depth // LANES, COMPS * steps, LANES), jnp.bfloat16),
            pltpu.VMEM((4, width, LANES), jnp.float32),
        ),
        in_specs=[SMEM] + [VMEM] * 5,
        out_specs=(VMEM, VMEM),
        scratch_shapes=[
            pltpu.VMEM((4, width // LANES, steps + 2 * ROWS, LANES), jnp.float32),
            pltpu.VMEM((width // LANES, 2 * COMPS, steps + ROWS, LANES), jnp.float32),
        ],
        compiler_params=pltpu.CompilerParams(vmem_limit_bytes=16 << 20),
        name="terms",
    )(edge, flow, near_core(low), near_core(high), area_vec, point_pos)
    pair = 2
    sums = pl.pallas_call(
        pair_kernel,
        out_shape=pltpu.VMEM((groups, steps, lanes), jnp.float32),
        in_specs=[VMEM] * 3,
        out_specs=VMEM,
        scratch_shapes=[
            pltpu.VMEM((2, groups, lanes), jnp.float32),
            pltpu.VMEM((3, groups, lanes), jnp.float32),
            pltpu.VMEM((pair, depth // 2, lanes), jnp.bfloat16),
            pltpu.VMEM((pair, depth // 2, lanes), jnp.bfloat16),
            pltpu.VMEM((COMPS * steps, pair * lanes), jnp.float32),
        ],
        compiler_params=pltpu.CompilerParams(vmem_limit_bytes=24 << 20),
        name="pairs",
    )(near_core(angles), near_core(terms), near_core(spread))
    sums = lax.all_to_all(sums, "obs", 0, 0, tiled=True)
    offsets = lax.dynamic_index_in_dim(band_offset, lax.axis_index("obs"), 0, keepdims=False)
    out, later = pl.pallas_call(
        place_kernel,
        out_shape=(pltpu.VMEM((steps, lanes), jnp.float32),) * 2,
        in_specs=[SMEM, VMEM],
        out_specs=(VMEM, VMEM),
        scratch_shapes=[pltpu.VMEM((2 * steps, lanes), jnp.float32)],
        compiler_params=pltpu.CompilerParams(vmem_limit_bytes=8 << 20),
        name="place",
    )(offsets, near_core(sums))
    carried = lax.ppermute(later, "tm", [(i, i + 1) for i in range(times - 1)])
    return out + carried


def solution(mesh):
    in_specs = (P(None, "tm", "obs"), P(None, "obs"), P(None, "obs"), P(None, "obs"), P())
    out_specs = P("tm", "obs")
    return jax.shard_map(local, mesh=mesh, in_specs=in_specs, out_specs=out_specs, check_vma=False)
```

```python
import math

import jax
import jax.numpy as jnp
from jax import lax
from jax.experimental import pallas as pl
from jax.experimental.pallas import tpu as pltpu
from jax.sharding import PartitionSpec as P


LAGS = 4
NEAR_RANGE = 3.25
SOUND_STEP = 1.17
RADIUS = 5.0 / SOUND_STEP
NEAREST = NEAR_RANGE / SOUND_STEP
SCALE = 1.0 / (4.0 * math.pi * SOUND_STEP * SOUND_STEP)
COMPS = 4
ROWS = 8
LANES = 128
CHUNK = 16
PARTS = 16


def prep_kernel(flow_ref, angle_ref, wide_ref, low_ref, high_ref, edges_ref, sem):
    steps = flow_ref.shape[1]
    copies = [
        pltpu.make_async_copy(flow_ref.at[:, pl.ds(start, ROWS), :], edges_ref.at[side], sem.at[side])
        for side, start in enumerate((steps - ROWS, 0))
    ]
    copies += [
        pltpu.make_async_copy(angle_ref, wide_ref.at[group], sem.at[2 + group]) for group in range(wide_ref.shape[0])
    ]
    for copy in copies:
        copy.start()
    for copy in copies[:2]:
        copy.wait()
    low_ref[...] = edges_ref[0, :, ROWS - LAGS :, :]
    high_ref[...] = edges_ref[1, :, :1, :]
    for copy in copies[2:]:
        copy.wait()


def terms_kernel(edge_ref, own_ref, flow_ref, low_ref, high_ref, area_ref, point_ref, terms_ref, spread_ref, field_ref, part_ref):
    steps = flow_ref.shape[1]
    width = flow_ref.shape[2]
    count = steps + ROWS
    for cut in range(width // LANES):
        lanes = slice(cut * LANES, (cut + 1) * LANES)
        area = [area_ref[i : i + 1, lanes] for i in range(3)]
        point = [(1.0 / SOUND_STEP) * point_ref[i : i + 1, lanes] for i in range(3)]

        def fields(source, start, rows):
            density = 1.0 + 0.2 * source[0, :, lanes]
            velocity = [0.4 * source[1 + i, :, lanes] for i in range(3)]
            pressure = source[4, :, lanes]
            normal_flux = velocity[0] * area[0] + velocity[1] * area[1] + velocity[2] * area[2]
            mass_flux = density * normal_flux
            field_ref[0, cut, start : start + rows, :] = mass_flux
            for i in range(3):
                field_ref[1 + i, cut, start : start + rows, :] = pressure * area[i] + mass_flux * velocity[i]

        field_ref[:, cut, ROWS + steps :, :] = jnp.zeros((4, ROWS, LANES), jnp.float32)
        fields(low_ref, ROWS - LAGS, LAGS)
        fields(flow_ref, ROWS, steps)
        fields(high_ref, ROWS + steps, 1)
        first = ROWS - LAGS + 1
        row = lax.broadcasted_iota(jnp.int32, (count, LANES), 0)
        keep = jnp.where(jnp.logical_or(row >= LAGS - 1, edge_ref[0] != 0), 1.0, 0.0)
        rates = [
            (0.5 * keep)
            * (field_ref[k, cut, first + 1 : first + 1 + count, :] - field_ref[k, cut, first - 1 : first - 1 + count, :])
            for k in range(4)
        ]
        loads = [keep * field_ref[1 + i, cut, first : first + count, :] for i in range(3)]
        reach = RADIUS * RADIUS + point[0] * point[0] + point[1] * point[1] + point[2] * point[2]
        mass_rate = SOUND_STEP * rates[0]
        far = rates[1:] + [-(point[0] * rates[1] + point[1] * rates[2] + point[2] * rates[3])]
        near = [loads[i] - (2.0 * point[i]) * mass_rate for i in range(3)]
        near.append(reach * mass_rate - (point[0] * loads[0] + point[1] * loads[1] + point[2] * loads[2]))
        for family, parts in enumerate((far, near)):
            for comp, part in enumerate(parts):
                part_ref[cut, family * COMPS + comp] = part
        for family in range(2):
            for comp in range(COMPS):
                for lag in range(LAGS):
                    start = LAGS - 1 - lag
                    block = (cut * 2 + family) * LAGS + lag
                    terms_ref[block, comp * steps : (comp + 1) * steps, :] = part_ref[
                        cut, family * COMPS + comp, start : start + steps, :
                    ].astype(jnp.bfloat16)
        turned = jnp.transpose(
            jnp.concatenate([2.0 * point[0], 2.0 * point[1], 2.0 * point[2], reach] * 2, axis=0)
        )
        for i in range(4):
            spread_ref[i, lanes, :] = jnp.broadcast_to(turned[:, i : i + 1], (LANES, LANES))


def fill_weights(places, spread_ref, weights_ref, part):
    span = spread_ref.shape[1]
    for start in range(span * part // PARTS, span * (part + 1) // PARTS, CHUNK):
        rows = slice(start, start + CHUNK)
        spread = [spread_ref[i, rows, :] for i in range(4)]
        for group, place in enumerate(places):
            square = spread[3] - place[0] * spread[0] - place[1] * spread[1] - place[2] * spread[2]
            inverse = lax.rsqrt(square)
            behind = (1.0 + NEAREST) - square * inverse
            first = jnp.maximum(behind, 0.0)
            passed = first - behind
            last = jnp.maximum(passed - 1.0, 0.0)
            middle = jnp.minimum(passed, 1.0)
            tents = (first, (1.0 - middle) - first, middle - last, last)
            far = inverse * inverse
            near = far * inverse
            quarter = start // LANES
            for family, coeff in enumerate((far, near)):
                for index, tent in enumerate(tents):
                    base = ((quarter * 2 + family) * LAGS + index) * LANES + start % LANES
                    weights_ref[group, base : base + CHUNK, :] = (coeff * tent).astype(jnp.bfloat16)


def sine_cosine(angle):
    half = 0.5 * angle
    square = half * half
    sine = cosine = 0.0
    for k in range(7, -1, -1):
        cosine = cosine * square + (-1.0) ** k / math.factorial(2 * k)
        sine = sine * square + (-1.0) ** k / math.factorial(2 * k + 1)
    sine = half * sine
    return 2.0 * sine * cosine, 1.0 - 2.0 * sine * sine


def pair_kernel(angle_ref, terms_ref, spread_ref, sums_ref, angles_ref, places_ref, even_ref, odd_ref, held_ref, rest_ref):
    groups, steps, lanes = sums_ref.shape
    for group in range(groups):
        for i in range(2):
            angles_ref[i, group : group + 1, :] = angle_ref[group, i : i + 1, :]
    sine, cosine = sine_cosine(angles_ref[0])
    rise, flat = sine_cosine(angles_ref[1])
    places_ref[0] = RADIUS * (cosine * flat)
    places_ref[1] = RADIUS * (sine * flat)
    places_ref[2] = RADIUS * rise
    pair = even_ref.shape[0]
    turns = groups // pair
    blocks = terms_ref.shape[0]

    def places_of(turn):
        return [[places_ref[i, pl.ds(turn * pair + j, 1), :] for i in range(3)] for j in range(pair)]

    def multiply(weights_ref, make):
        total = None
        for part in range(PARTS):
            span = range(blocks * part // PARTS, blocks * (part + 1) // PARTS)
            terms = jnp.concatenate([terms_ref[k] for k in span], axis=1)
            rows = slice(span[0] * LANES, (span[-1] + 1) * LANES)
            weights = jnp.concatenate([weights_ref[j, rows, :] for j in range(pair)], axis=1)
            piece = jnp.dot(terms, weights, preferred_element_type=jnp.float32)
            total = piece if total is None else total + piece
            make(part)
        return total

    def finish(turn, total_ref):
        for j, place in enumerate(places_of(turn)):
            mine = total_ref[:, j * lanes : (j + 1) * lanes]
            result = mine[3 * steps :]
            for i in range(3):
                result = result + place[i] * mine[i * steps : (i + 1) * steps]
            sums_ref[turn * pair + j] = SCALE * result

    for part in range(PARTS):
        fill_weights(places_of(0), spread_ref, even_ref, part)

    def body(step, carry):
        even = 2 * step
        odd = 2 * step + 1

        @pl.when(step >= 0)
        def _():
            finish(jnp.maximum(even - 1, 0), rest_ref)
            places = places_of(odd)
            held_ref[...] = multiply(even_ref, lambda part: fill_weights(places, spread_ref, odd_ref, part))

        @pl.when(odd < turns - 1)
        def _():
            finish(even, held_ref)
            places = places_of(odd + 1)
            rest_ref[...] = multiply(odd_ref, lambda part: fill_weights(places, spread_ref, even_ref, part))

        return carry

    lax.fori_loop(0, turns // 2, body, 0)
    finish(turns - 2, held_ref)
    rest_ref[...] = multiply(odd_ref, lambda part: None)
    finish(turns - 1, rest_ref)


def place_kernel(own_ref, offset_ref, sums_ref, out_ref, later_ref, canvas_ref):
    groups, steps, _ = sums_ref.shape
    canvas_ref[...] = jnp.zeros_like(canvas_ref)
    for block in range(groups):
        span = pl.ds(offset_ref[own_ref[0], block], steps)
        canvas_ref[span, :] = canvas_ref[span, :] + sums_ref[block]
    out_ref[...] = canvas_ref[:steps]
    later_ref[...] = canvas_ref[steps : 2 * steps]


VMEM = pl.BlockSpec(memory_space=pltpu.VMEM)
SMEM = pl.BlockSpec(memory_space=pltpu.SMEM)
HBM = pl.BlockSpec(memory_space=pltpu.HBM)


def near_core(array):
    return pltpu.with_memory_space_constraint(array, pltpu.VMEM)


def in_hbm(array):
    return pltpu.with_memory_space_constraint(array, pltpu.HBM)


def local(flow, point_pos, area_vec, observer_angles, band_offset):
    steps = flow.shape[1]
    width = flow.shape[2]
    groups = lax.axis_size("obs")
    lanes = observer_angles.shape[1]
    times = lax.axis_size("tm")
    wide, low, high = pl.pallas_call(
        prep_kernel,
        out_shape=(
            jax.ShapeDtypeStruct((groups, 2, lanes), jnp.float32),
            pltpu.VMEM((5, LAGS, width), jnp.float32),
            pltpu.VMEM((5, 1, width), jnp.float32),
        ),
        in_specs=[HBM, HBM],
        out_specs=(HBM, VMEM, VMEM),
        scratch_shapes=[pltpu.VMEM((2, 5, ROWS, width), jnp.float32), pltpu.SemaphoreType.DMA((2 + groups,))],
        compiler_params=pltpu.CompilerParams(vmem_limit_bytes=8 << 20),
        name="prep",
    )(in_hbm(flow), in_hbm(observer_angles))
    angles = lax.all_to_all(wide, "obs", 0, 0, tiled=True)
    low = lax.ppermute(low, "tm", [(i, i + 1) for i in range(times - 1)])
    high = lax.ppermute(high, "tm", [(i + 1, i) for i in range(times - 1)])
    edge = lax.axis_index("tm").astype(jnp.int32).reshape(1)
    own = lax.axis_index("obs").astype(jnp.int32).reshape(1)
    depth = 2 * LAGS * width
    terms, spread = pl.pallas_call(
        terms_kernel,
        out_shape=(
            pltpu.VMEM((depth // LANES, COMPS * steps, LANES), jnp.bfloat16),
            pltpu.VMEM((4, width, LANES), jnp.float32),
        ),
        in_specs=[SMEM] * 2 + [VMEM] * 5,
        out_specs=(VMEM, VMEM),
        scratch_shapes=[
            pltpu.VMEM((4, width // LANES, steps + 2 * ROWS, LANES), jnp.float32),
            pltpu.VMEM((width // LANES, 2 * COMPS, steps + ROWS, LANES), jnp.float32),
        ],
        compiler_params=pltpu.CompilerParams(vmem_limit_bytes=16 << 20),
        name="terms",
    )(edge, own, in_hbm(flow), near_core(low), near_core(high), in_hbm(area_vec), in_hbm(point_pos))
    pair = 2
    sums = pl.pallas_call(
        pair_kernel,
        out_shape=pltpu.VMEM((groups, steps, lanes), jnp.float32),
        in_specs=[VMEM] * 3,
        out_specs=VMEM,
        scratch_shapes=[
            pltpu.VMEM((2, groups, lanes), jnp.float32),
            pltpu.VMEM((3, groups, lanes), jnp.float32),
            pltpu.VMEM((pair, depth, lanes), jnp.bfloat16),
            pltpu.VMEM((pair, depth, lanes), jnp.bfloat16),
            pltpu.VMEM((COMPS * steps, pair * lanes), jnp.float32),
            pltpu.VMEM((COMPS * steps, pair * lanes), jnp.float32),
        ],
        compiler_params=pltpu.CompilerParams(vmem_limit_bytes=24 << 20),
        name="pairs",
    )(near_core(angles), near_core(terms), near_core(spread))
    sums = lax.all_to_all(sums, "obs", 0, 0, tiled=True)
    out, later = pl.pallas_call(
        place_kernel,
        out_shape=(pltpu.VMEM((steps, lanes), jnp.float32),) * 2,
        in_specs=[SMEM, SMEM, VMEM],
        out_specs=(VMEM, VMEM),
        scratch_shapes=[pltpu.VMEM((2 * steps, lanes), jnp.float32)],
        compiler_params=pltpu.CompilerParams(vmem_limit_bytes=8 << 20),
        name="place",
    )(own, band_offset, near_core(sums))
    carried = lax.ppermute(later, "tm", [(i, i + 1) for i in range(times - 1)])
    return out + carried


def solution(mesh):
    in_specs = (P(None, "tm", "obs"), P(None, "obs"), P(None, "obs"), P(None, "obs"), P())
    out_specs = P("tm", "obs")
    return jax.shard_map(local, mesh=mesh, in_specs=in_specs, out_specs=out_specs, check_vma=False)
```

```python
import math

import jax
import jax.numpy as jnp
from jax import lax
from jax.experimental import pallas as pl
from jax.experimental.pallas import tpu as pltpu
from jax.sharding import PartitionSpec as P


LAGS = 4
NEAR_RANGE = 3.25
SOUND_STEP = 1.17
RADIUS = 5.0 / SOUND_STEP
NEAREST = NEAR_RANGE / SOUND_STEP
SCALE = 1.0 / (4.0 * math.pi * SOUND_STEP * SOUND_STEP)
COMPS = 4
ROWS = 8
LANES = 128
CHUNK = 16
PARTS = 16


def prep_kernel(flow_ref, angle_ref, wide_ref, low_ref, high_ref, edges_ref, held_ref, spread_ref, sem):
    steps = flow_ref.shape[1]
    inward = pltpu.make_async_copy(angle_ref, held_ref, sem.at[2])
    inward.start()
    copies = [
        pltpu.make_async_copy(flow_ref.at[:, pl.ds(start, ROWS), :], edges_ref.at[side], sem.at[side])
        for side, start in enumerate((steps - ROWS, 0))
    ]
    for copy in copies:
        copy.start()
    inward.wait()
    for group in range(spread_ref.shape[0]):
        spread_ref[group] = held_ref[...]
    outward = pltpu.make_async_copy(spread_ref, wide_ref, sem.at[3])
    outward.start()
    for copy in copies:
        copy.wait()
    low_ref[...] = edges_ref[0, :, ROWS - LAGS :, :]
    high_ref[...] = edges_ref[1, :, :1, :]
    outward.wait()


def terms_kernel(edge_ref, own_ref, flow_ref, low_ref, high_ref, area_ref, point_ref, terms_ref, spread_ref, field_ref, part_ref):
    steps = flow_ref.shape[1]
    width = flow_ref.shape[2]
    count = steps + ROWS
    for cut in range(width // LANES):
        lanes = slice(cut * LANES, (cut + 1) * LANES)
        area = [area_ref[i : i + 1, lanes] for i in range(3)]
        point = [(1.0 / SOUND_STEP) * point_ref[i : i + 1, lanes] for i in range(3)]

        def fields(source, start, rows):
            density = 1.0 + 0.2 * source[0, :, lanes]
            velocity = [0.4 * source[1 + i, :, lanes] for i in range(3)]
            pressure = source[4, :, lanes]
            normal_flux = velocity[0] * area[0] + velocity[1] * area[1] + velocity[2] * area[2]
            mass_flux = density * normal_flux
            field_ref[0, cut, start : start + rows, :] = mass_flux
            for i in range(3):
                field_ref[1 + i, cut, start : start + rows, :] = pressure * area[i] + mass_flux * velocity[i]

        field_ref[:, cut, ROWS + steps :, :] = jnp.zeros((4, ROWS, LANES), jnp.float32)
        fields(low_ref, ROWS - LAGS, LAGS)
        fields(flow_ref, ROWS, steps)
        fields(high_ref, ROWS + steps, 1)
        first = ROWS - LAGS + 1
        row = lax.broadcasted_iota(jnp.int32, (count, LANES), 0)
        keep = jnp.where(jnp.logical_or(row >= LAGS - 1, edge_ref[0] != 0), 1.0, 0.0)
        rates = [
            (0.5 * keep)
            * (field_ref[k, cut, first + 1 : first + 1 + count, :] - field_ref[k, cut, first - 1 : first - 1 + count, :])
            for k in range(4)
        ]
        loads = [keep * field_ref[1 + i, cut, first : first + count, :] for i in range(3)]
        reach = RADIUS * RADIUS + point[0] * point[0] + point[1] * point[1] + point[2] * point[2]
        mass_rate = SOUND_STEP * rates[0]
        far = rates[1:] + [-(point[0] * rates[1] + point[1] * rates[2] + point[2] * rates[3])]
        near = [loads[i] - (2.0 * point[i]) * mass_rate for i in range(3)]
        near.append(reach * mass_rate - (point[0] * loads[0] + point[1] * loads[1] + point[2] * loads[2]))
        for family, parts in enumerate((far, near)):
            for comp, part in enumerate(parts):
                part_ref[cut, family * COMPS + comp] = part
        for family in range(2):
            for comp in range(COMPS):
                for lag in range(LAGS):
                    start = LAGS - 1 - lag
                    block = (cut * 2 + family) * LAGS + lag
                    terms_ref[block, comp * steps : (comp + 1) * steps, :] = part_ref[
                        cut, family * COMPS + comp, start : start + steps, :
                    ].astype(jnp.bfloat16)
        turned = jnp.transpose(
            jnp.concatenate([2.0 * point[0], 2.0 * point[1], 2.0 * point[2], reach] * 2, axis=0)
        )
        for i in range(4):
            spread_ref[i, lanes, :] = jnp.broadcast_to(turned[:, i : i + 1], (LANES, LANES))


def fill_weights(places, spread_ref, weights_ref, part):
    span = spread_ref.shape[1]
    for start in range(span * part // PARTS, span * (part + 1) // PARTS, CHUNK):
        rows = slice(start, start + CHUNK)
        spread = [spread_ref[i, rows, :] for i in range(4)]
        for group, place in enumerate(places):
            square = spread[3] - place[0] * spread[0] - place[1] * spread[1] - place[2] * spread[2]
            inverse = lax.rsqrt(square)
            behind = (1.0 + NEAREST) - square * inverse
            first = jnp.maximum(behind, 0.0)
            passed = first - behind
            last = jnp.maximum(passed - 1.0, 0.0)
            middle = jnp.minimum(passed, 1.0)
            tents = (first, (1.0 - middle) - first, middle - last, last)
            far = inverse * inverse
            near = far * inverse
            quarter = start // LANES
            for family, coeff in enumerate((far, near)):
                for index, tent in enumerate(tents):
                    base = ((quarter * 2 + family) * LAGS + index) * LANES + start % LANES
                    weights_ref[group, base : base + CHUNK, :] = (coeff * tent).astype(jnp.bfloat16)


def sine_cosine(angle):
    half = 0.5 * angle
    square = half * half
    sine = cosine = 0.0
    for k in range(7, -1, -1):
        cosine = cosine * square + (-1.0) ** k / math.factorial(2 * k)
        sine = sine * square + (-1.0) ** k / math.factorial(2 * k + 1)
    sine = half * sine
    return 2.0 * sine * cosine, 1.0 - 2.0 * sine * sine


def pair_kernel(angle_ref, terms_ref, spread_ref, sums_ref, angles_ref, places_ref, even_ref, odd_ref, held_ref, rest_ref):
    groups, steps, lanes = sums_ref.shape
    for group in range(groups):
        for i in range(2):
            angles_ref[i, group : group + 1, :] = angle_ref[group, i : i + 1, :]
    sine, cosine = sine_cosine(angles_ref[0])
    rise, flat = sine_cosine(angles_ref[1])
    places_ref[0] = RADIUS * (cosine * flat)
    places_ref[1] = RADIUS * (sine * flat)
    places_ref[2] = RADIUS * rise
    pair = even_ref.shape[0]
    turns = groups // pair
    blocks = terms_ref.shape[0]

    def places_of(turn):
        return [[places_ref[i, pl.ds(turn * pair + j, 1), :] for i in range(3)] for j in range(pair)]

    def multiply(weights_ref, make):
        total = None
        for part in range(PARTS):
            span = range(blocks * part // PARTS, blocks * (part + 1) // PARTS)
            terms = jnp.concatenate([terms_ref[k] for k in span], axis=1)
            rows = slice(span[0] * LANES, (span[-1] + 1) * LANES)
            weights = jnp.concatenate([weights_ref[j, rows, :] for j in range(pair)], axis=1)
            piece = jnp.dot(terms, weights, preferred_element_type=jnp.float32)
            total = piece if total is None else total + piece
            make(part)
        return total

    def finish(turn, total_ref):
        for j, place in enumerate(places_of(turn)):
            mine = total_ref[:, j * lanes : (j + 1) * lanes]
            result = mine[3 * steps :]
            for i in range(3):
                result = result + place[i] * mine[i * steps : (i + 1) * steps]
            sums_ref[turn * pair + j] = (SCALE * result).astype(sums_ref.dtype)

    for part in range(PARTS):
        fill_weights(places_of(0), spread_ref, even_ref, part)

    def body(step, carry):
        even = 2 * step
        odd = 2 * step + 1

        @pl.when(step >= 0)
        def _():
            finish(jnp.maximum(even - 1, 0), rest_ref)
            places = places_of(odd)
            held_ref[...] = multiply(even_ref, lambda part: fill_weights(places, spread_ref, odd_ref, part))

        @pl.when(odd < turns - 1)
        def _():
            finish(even, held_ref)
            places = places_of(odd + 1)
            rest_ref[...] = multiply(odd_ref, lambda part: fill_weights(places, spread_ref, even_ref, part))

        return carry

    lax.fori_loop(0, turns // 2, body, 0)
    finish(turns - 2, held_ref)
    rest_ref[...] = multiply(odd_ref, lambda part: None)
    finish(turns - 1, rest_ref)


def place_kernel(own_ref, offset_ref, sums_ref, out_ref, later_ref, canvas_ref):
    groups, steps, _ = sums_ref.shape
    canvas_ref[...] = jnp.zeros_like(canvas_ref)
    for block in range(groups):
        span = pl.ds(offset_ref[own_ref[0], block], steps)
        canvas_ref[span, :] = canvas_ref[span, :] + sums_ref[block].astype(jnp.float32)
    out_ref[...] = canvas_ref[:steps]
    later_ref[...] = canvas_ref[steps : 2 * steps]


VMEM = pl.BlockSpec(memory_space=pltpu.VMEM)
SMEM = pl.BlockSpec(memory_space=pltpu.SMEM)
HBM = pl.BlockSpec(memory_space=pltpu.HBM)


def near_core(array):
    return pltpu.with_memory_space_constraint(array, pltpu.VMEM)


def in_hbm(array):
    return pltpu.with_memory_space_constraint(array, pltpu.HBM)


def local(flow, point_pos, area_vec, observer_angles, band_offset):
    steps = flow.shape[1]
    width = flow.shape[2]
    groups = lax.axis_size("obs")
    lanes = observer_angles.shape[1]
    times = lax.axis_size("tm")
    wide, low, high = pl.pallas_call(
        prep_kernel,
        out_shape=(
            jax.ShapeDtypeStruct((groups, 2, lanes), jnp.float32),
            pltpu.VMEM((5, LAGS, width), jnp.float32),
            pltpu.VMEM((5, 1, width), jnp.float32),
        ),
        in_specs=[HBM, HBM],
        out_specs=(HBM, VMEM, VMEM),
        scratch_shapes=[
            pltpu.VMEM((2, 5, ROWS, width), jnp.float32),
            pltpu.VMEM((2, lanes), jnp.float32),
            pltpu.VMEM((groups, 2, lanes), jnp.float32),
            pltpu.SemaphoreType.DMA((4,)),
        ],
        compiler_params=pltpu.CompilerParams(vmem_limit_bytes=8 << 20),
        name="prep",
    )(in_hbm(flow), in_hbm(observer_angles))
    angles = lax.all_to_all(wide, "obs", 0, 0, tiled=True)
    low = lax.ppermute(low, "tm", [(i, i + 1) for i in range(times - 1)])
    high = lax.ppermute(high, "tm", [(i + 1, i) for i in range(times - 1)])
    edge = lax.axis_index("tm").astype(jnp.int32).reshape(1)
    own = lax.axis_index("obs").astype(jnp.int32).reshape(1)
    depth = 2 * LAGS * width
    terms, spread = pl.pallas_call(
        terms_kernel,
        out_shape=(
            pltpu.VMEM((depth // LANES, COMPS * steps, LANES), jnp.bfloat16),
            pltpu.VMEM((4, width, LANES), jnp.float32),
        ),
        in_specs=[SMEM] * 2 + [VMEM] * 5,
        out_specs=(VMEM, VMEM),
        scratch_shapes=[
            pltpu.VMEM((4, width // LANES, steps + 2 * ROWS, LANES), jnp.float32),
            pltpu.VMEM((width // LANES, 2 * COMPS, steps + ROWS, LANES), jnp.float32),
        ],
        compiler_params=pltpu.CompilerParams(vmem_limit_bytes=16 << 20),
        name="terms",
    )(edge, own, in_hbm(flow), near_core(low), near_core(high), in_hbm(area_vec), in_hbm(point_pos))
    pair = 2
    sums = pl.pallas_call(
        pair_kernel,
        out_shape=pltpu.VMEM((groups, steps, lanes), jnp.bfloat16),
        in_specs=[VMEM] * 3,
        out_specs=VMEM,
        scratch_shapes=[
            pltpu.VMEM((2, groups, lanes), jnp.float32),
            pltpu.VMEM((3, groups, lanes), jnp.float32),
            pltpu.VMEM((pair, depth, lanes), jnp.bfloat16),
            pltpu.VMEM((pair, depth, lanes), jnp.bfloat16),
            pltpu.VMEM((COMPS * steps, pair * lanes), jnp.float32),
            pltpu.VMEM((COMPS * steps, pair * lanes), jnp.float32),
        ],
        compiler_params=pltpu.CompilerParams(vmem_limit_bytes=24 << 20),
        name="pairs",
    )(near_core(angles), near_core(terms), near_core(spread))
    sums = lax.all_to_all(sums, "obs", 0, 0, tiled=True)
    out, later = pl.pallas_call(
        place_kernel,
        out_shape=(pltpu.VMEM((steps, lanes), jnp.float32),) * 2,
        in_specs=[SMEM, SMEM, VMEM],
        out_specs=(VMEM, VMEM),
        scratch_shapes=[pltpu.VMEM((2 * steps, lanes), jnp.float32)],
        compiler_params=pltpu.CompilerParams(vmem_limit_bytes=8 << 20),
        name="place",
    )(own, band_offset, near_core(sums))
    carried = lax.ppermute(later, "tm", [(i, i + 1) for i in range(times - 1)])
    return out + carried


def solution(mesh):
    in_specs = (P(None, "tm", "obs"), P(None, "obs"), P(None, "obs"), P(None, "obs"), P())
    out_specs = P("tm", "obs")
    return jax.shard_map(local, mesh=mesh, in_specs=in_specs, out_specs=out_specs, check_vma=False)
```

```python
import math

import jax
import jax.numpy as jnp
from jax import lax
from jax.experimental import pallas as pl
from jax.experimental.pallas import tpu as pltpu
from jax.sharding import PartitionSpec as P


LAGS = 4
NEAR_RANGE = 3.25
SOUND_STEP = 1.17
RADIUS = 5.0 / SOUND_STEP
NEAREST = NEAR_RANGE / SOUND_STEP
SCALE = 1.0 / (4.0 * math.pi * SOUND_STEP * SOUND_STEP)
COMPS = 4
ROWS = 8
LANES = 128
CHUNK = 16
PARTS = 16


def prep_kernel(time_ref, flow_ref, angle_ref, wide_ref, core_ref, chip_ref, edges_ref, held_ref, spread_ref, sem):
    steps = flow_ref.shape[1]
    inward = pltpu.make_async_copy(angle_ref, held_ref, sem.at[2])
    inward.start()
    copies = [
        pltpu.make_async_copy(flow_ref.at[:, pl.ds(start, ROWS), :], edges_ref.at[side], sem.at[side])
        for side, start in enumerate((steps - ROWS, 0))
    ]
    for copy in copies:
        copy.start()
    inward.wait()
    for group in range(spread_ref.shape[0]):
        spread_ref[group] = held_ref[...]
    outward = pltpu.make_async_copy(spread_ref, wide_ref, sem.at[3])
    outward.start()
    for copy in copies:
        copy.wait()
    even = time_ref[0] % 2 == 0
    last = edges_ref[0, :, ROWS - LAGS :, :]
    first = edges_ref[1, :, :LAGS, :]
    core_ref[...] = jnp.where(even, last, first)
    chip_ref[...] = jnp.where(even, first, last)
    outward.wait()


def terms_kernel(time_ref, own_ref, flow_ref, core_ref, chip_ref, area_ref, point_ref, terms_ref, spread_ref, field_ref, part_ref):
    steps = flow_ref.shape[1]
    width = flow_ref.shape[2]
    count = steps + ROWS
    even = time_ref[0] % 2 == 0
    low = jnp.where(even, chip_ref[...], core_ref[...])
    high = jnp.where(even, core_ref[:, :1, :], chip_ref[:, :1, :])
    for cut in range(width // LANES):
        lanes = slice(cut * LANES, (cut + 1) * LANES)
        area = [area_ref[i : i + 1, lanes] for i in range(3)]
        point = [(1.0 / SOUND_STEP) * point_ref[i : i + 1, lanes] for i in range(3)]

        def fields(source, start, rows):
            density = 1.0 + 0.2 * source[0, :, lanes]
            velocity = [0.4 * source[1 + i, :, lanes] for i in range(3)]
            pressure = source[4, :, lanes]
            normal_flux = velocity[0] * area[0] + velocity[1] * area[1] + velocity[2] * area[2]
            mass_flux = density * normal_flux
            field_ref[0, cut, start : start + rows, :] = mass_flux
            for i in range(3):
                field_ref[1 + i, cut, start : start + rows, :] = pressure * area[i] + mass_flux * velocity[i]

        field_ref[:, cut, ROWS + steps :, :] = jnp.zeros((4, ROWS, LANES), jnp.float32)
        fields(low, ROWS - LAGS, LAGS)
        fields(flow_ref, ROWS, steps)
        fields(high, ROWS + steps, 1)
        first = ROWS - LAGS + 1
        row = lax.broadcasted_iota(jnp.int32, (count, LANES), 0)
        keep = jnp.where(jnp.logical_or(row >= LAGS - 1, time_ref[0] != 0), 1.0, 0.0)
        rates = [
            (0.5 * keep)
            * (field_ref[k, cut, first + 1 : first + 1 + count, :] - field_ref[k, cut, first - 1 : first - 1 + count, :])
            for k in range(4)
        ]
        loads = [keep * field_ref[1 + i, cut, first : first + count, :] for i in range(3)]
        reach = RADIUS * RADIUS + point[0] * point[0] + point[1] * point[1] + point[2] * point[2]
        mass_rate = SOUND_STEP * rates[0]
        far = rates[1:] + [-(point[0] * rates[1] + point[1] * rates[2] + point[2] * rates[3])]
        near = [loads[i] - (2.0 * point[i]) * mass_rate for i in range(3)]
        near.append(reach * mass_rate - (point[0] * loads[0] + point[1] * loads[1] + point[2] * loads[2]))
        for family, parts in enumerate((far, near)):
            for comp, part in enumerate(parts):
                part_ref[cut, family * COMPS + comp] = part
        for family in range(2):
            for comp in range(COMPS):
                for lag in range(LAGS):
                    start = LAGS - 1 - lag
                    block = (cut * 2 + family) * LAGS + lag
                    terms_ref[block, comp * steps : (comp + 1) * steps, :] = part_ref[
                        cut, family * COMPS + comp, start : start + steps, :
                    ].astype(jnp.bfloat16)
        turned = jnp.transpose(
            jnp.concatenate([2.0 * point[0], 2.0 * point[1], 2.0 * point[2], reach] * 2, axis=0)
        )
        for i in range(4):
            spread_ref[i, lanes, :] = jnp.broadcast_to(turned[:, i : i + 1], (LANES, LANES))


def fill_weights(places, spread_ref, weights_ref, part):
    span = spread_ref.shape[1]
    for start in range(span * part // PARTS, span * (part + 1) // PARTS, CHUNK):
        rows = slice(start, start + CHUNK)
        spread = [spread_ref[i, rows, :] for i in range(4)]
        for group, place in enumerate(places):
            square = spread[3] - place[0] * spread[0] - place[1] * spread[1] - place[2] * spread[2]
            inverse = lax.rsqrt(square)
            behind = (1.0 + NEAREST) - square * inverse
            first = jnp.maximum(behind, 0.0)
            passed = first - behind
            last = jnp.maximum(passed - 1.0, 0.0)
            middle = jnp.minimum(passed, 1.0)
            tents = (first, (1.0 - middle) - first, middle - last, last)
            far = inverse * inverse
            near = far * inverse
            quarter = start // LANES
            for family, coeff in enumerate((far, near)):
                for index, tent in enumerate(tents):
                    base = ((quarter * 2 + family) * LAGS + index) * LANES + start % LANES
                    weights_ref[group, base : base + CHUNK, :] = (coeff * tent).astype(jnp.bfloat16)


def sine_cosine(angle):
    half = 0.5 * angle
    square = half * half
    sine = cosine = 0.0
    for k in range(7, -1, -1):
        cosine = cosine * square + (-1.0) ** k / math.factorial(2 * k)
        sine = sine * square + (-1.0) ** k / math.factorial(2 * k + 1)
    sine = half * sine
    return 2.0 * sine * cosine, 1.0 - 2.0 * sine * sine


def pair_kernel(angle_ref, terms_ref, spread_ref, sums_ref, angles_ref, places_ref, even_ref, odd_ref, held_ref, rest_ref):
    groups, steps, lanes = sums_ref.shape
    for group in range(groups):
        for i in range(2):
            angles_ref[i, group : group + 1, :] = angle_ref[group, i : i + 1, :]
    sine, cosine = sine_cosine(angles_ref[0])
    rise, flat = sine_cosine(angles_ref[1])
    places_ref[0] = RADIUS * (cosine * flat)
    places_ref[1] = RADIUS * (sine * flat)
    places_ref[2] = RADIUS * rise
    pair = even_ref.shape[0]
    turns = groups // pair
    blocks = terms_ref.shape[0]

    def places_of(turn):
        return [[places_ref[i, pl.ds(turn * pair + j, 1), :] for i in range(3)] for j in range(pair)]

    def multiply(weights_ref, make):
        total = None
        for part in range(PARTS):
            span = range(blocks * part // PARTS, blocks * (part + 1) // PARTS)
            terms = jnp.concatenate([terms_ref[k] for k in span], axis=1)
            rows = slice(span[0] * LANES, (span[-1] + 1) * LANES)
            weights = jnp.concatenate([weights_ref[j, rows, :] for j in range(pair)], axis=1)
            piece = jnp.dot(terms, weights, preferred_element_type=jnp.float32)
            total = piece if total is None else total + piece
            make(part)
        return total

    def finish(turn, total_ref):
        for j, place in enumerate(places_of(turn)):
            mine = total_ref[:, j * lanes : (j + 1) * lanes]
            result = mine[3 * steps :]
            for i in range(3):
                result = result + place[i] * mine[i * steps : (i + 1) * steps]
            sums_ref[turn * pair + j] = (SCALE * result).astype(sums_ref.dtype)

    for part in range(PARTS):
        fill_weights(places_of(0), spread_ref, even_ref, part)

    def body(step, carry):
        even = 2 * step
        odd = 2 * step + 1

        @pl.when(step >= 0)
        def _():
            finish(jnp.maximum(even - 1, 0), rest_ref)
            places = places_of(odd)
            held_ref[...] = multiply(even_ref, lambda part: fill_weights(places, spread_ref, odd_ref, part))

        @pl.when(odd < turns - 1)
        def _():
            finish(even, held_ref)
            places = places_of(odd + 1)
            rest_ref[...] = multiply(odd_ref, lambda part: fill_weights(places, spread_ref, even_ref, part))

        return carry

    lax.fori_loop(0, turns // 2, body, 0)
    finish(turns - 2, held_ref)
    rest_ref[...] = multiply(odd_ref, lambda part: None)
    finish(turns - 1, rest_ref)


def place_kernel(own_ref, offset_ref, sums_ref, out_ref, later_ref, canvas_ref):
    groups, steps, _ = sums_ref.shape
    canvas_ref[...] = jnp.zeros_like(canvas_ref)
    for block in range(groups):
        span = pl.ds(offset_ref[own_ref[0], block], steps)
        canvas_ref[span, :] = canvas_ref[span, :] + sums_ref[block].astype(jnp.float32)
    out_ref[...] = canvas_ref[:steps]
    later_ref[...] = canvas_ref[steps : 2 * steps]


VMEM = pl.BlockSpec(memory_space=pltpu.VMEM)
SMEM = pl.BlockSpec(memory_space=pltpu.SMEM)
HBM = pl.BlockSpec(memory_space=pltpu.HBM)


def near_core(array):
    return pltpu.with_memory_space_constraint(array, pltpu.VMEM)


def in_hbm(array):
    return pltpu.with_memory_space_constraint(array, pltpu.HBM)


def local(flow, point_pos, area_vec, observer_angles, band_offset):
    steps = flow.shape[1]
    width = flow.shape[2]
    groups = lax.axis_size("obs")
    lanes = observer_angles.shape[1]
    times = lax.axis_size("tm")
    time = lax.axis_index("tm").astype(jnp.int32).reshape(1)
    wide, to_core, to_chip = pl.pallas_call(
        prep_kernel,
        out_shape=(
            jax.ShapeDtypeStruct((groups, 2, lanes), jnp.float32),
            pltpu.VMEM((5, LAGS, width), jnp.float32),
            pltpu.VMEM((5, LAGS, width), jnp.float32),
        ),
        in_specs=[SMEM, HBM, HBM],
        out_specs=(HBM, VMEM, VMEM),
        scratch_shapes=[
            pltpu.VMEM((2, 5, ROWS, width), jnp.float32),
            pltpu.VMEM((2, lanes), jnp.float32),
            pltpu.VMEM((groups, 2, lanes), jnp.float32),
            pltpu.SemaphoreType.DMA((4,)),
        ],
        compiler_params=pltpu.CompilerParams(vmem_limit_bytes=8 << 20),
        name="prep",
    )(time, in_hbm(flow), in_hbm(observer_angles))
    angles = lax.all_to_all(wide, "obs", 0, 0, tiled=True)
    from_core = lax.ppermute(to_core, "tm", [(i, i ^ 1) for i in range(times)])
    swaps = [(i, i + 1) for i in range(1, times - 1, 2)]
    from_chip = lax.ppermute(to_chip, "tm", swaps + [(j, i) for i, j in swaps])
    own = lax.axis_index("obs").astype(jnp.int32).reshape(1)
    depth = 2 * LAGS * width
    terms, spread = pl.pallas_call(
        terms_kernel,
        out_shape=(
            pltpu.VMEM((depth // LANES, COMPS * steps, LANES), jnp.bfloat16),
            pltpu.VMEM((4, width, LANES), jnp.float32),
        ),
        in_specs=[SMEM] * 2 + [VMEM] * 5,
        out_specs=(VMEM, VMEM),
        scratch_shapes=[
            pltpu.VMEM((4, width // LANES, steps + 2 * ROWS, LANES), jnp.float32),
            pltpu.VMEM((width // LANES, 2 * COMPS, steps + ROWS, LANES), jnp.float32),
        ],
        compiler_params=pltpu.CompilerParams(vmem_limit_bytes=16 << 20),
        name="terms",
    )(time, own, in_hbm(flow), near_core(from_core), near_core(from_chip), in_hbm(area_vec), in_hbm(point_pos))
    pair = 2
    sums = pl.pallas_call(
        pair_kernel,
        out_shape=pltpu.VMEM((groups, steps, lanes), jnp.bfloat16),
        in_specs=[VMEM] * 3,
        out_specs=VMEM,
        scratch_shapes=[
            pltpu.VMEM((2, groups, lanes), jnp.float32),
            pltpu.VMEM((3, groups, lanes), jnp.float32),
            pltpu.VMEM((pair, depth, lanes), jnp.bfloat16),
            pltpu.VMEM((pair, depth, lanes), jnp.bfloat16),
            pltpu.VMEM((COMPS * steps, pair * lanes), jnp.float32),
            pltpu.VMEM((COMPS * steps, pair * lanes), jnp.float32),
        ],
        compiler_params=pltpu.CompilerParams(vmem_limit_bytes=24 << 20),
        name="pairs",
    )(near_core(angles), near_core(terms), near_core(spread))
    sums = lax.all_to_all(sums, "obs", 0, 0, tiled=True)
    out, later = pl.pallas_call(
        place_kernel,
        out_shape=(pltpu.VMEM((steps, lanes), jnp.float32),) * 2,
        in_specs=[SMEM, SMEM, VMEM],
        out_specs=(VMEM, VMEM),
        scratch_shapes=[pltpu.VMEM((2 * steps, lanes), jnp.float32)],
        compiler_params=pltpu.CompilerParams(vmem_limit_bytes=8 << 20),
        name="place",
    )(own, band_offset, near_core(sums))
    carried = lax.ppermute(later, "tm", [(i, i + 1) for i in range(times - 1)])
    return out + carried


def solution(mesh):
    in_specs = (P(None, "tm", "obs"), P(None, "obs"), P(None, "obs"), P(None, "obs"), P())
    out_specs = P("tm", "obs")
    return jax.shard_map(local, mesh=mesh, in_specs=in_specs, out_specs=out_specs, check_vma=False)
```

```python
import math

import jax
import jax.numpy as jnp
from jax import lax
from jax.experimental import pallas as pl
from jax.experimental.pallas import tpu as pltpu
from jax.sharding import PartitionSpec as P


LAGS = 4
NEAR_RANGE = 3.25
SOUND_STEP = 1.17
RADIUS = 5.0 / SOUND_STEP
NEAREST = NEAR_RANGE / SOUND_STEP
SCALE = 1.0 / (4.0 * math.pi * SOUND_STEP * SOUND_STEP)
COMPS = 4
ROWS = 8
LANES = 128
CHUNK = 16
PARTS = 16


def prep_kernel(time_ref, flow_ref, angle_ref, wide_ref, core_ref, chip_ref, edges_ref, held_ref, spread_ref, sem):
    steps = flow_ref.shape[1]
    inward = pltpu.make_async_copy(angle_ref, held_ref, sem.at[2])
    inward.start()
    copies = [
        pltpu.make_async_copy(flow_ref.at[:, pl.ds(start, ROWS), :], edges_ref.at[side], sem.at[side])
        for side, start in enumerate((steps - ROWS, 0))
    ]
    for copy in copies:
        copy.start()
    inward.wait()
    for group in range(spread_ref.shape[0]):
        spread_ref[group] = held_ref[...]
    outward = pltpu.make_async_copy(spread_ref, wide_ref, sem.at[3])
    outward.start()
    for copy in copies:
        copy.wait()
    even = time_ref[0] % 2 == 0
    last = edges_ref[0, :, ROWS - LAGS :, :]
    first = edges_ref[1, :, :LAGS, :]
    core_ref[...] = jnp.where(even, last, first)
    chip_ref[...] = jnp.where(even, first, last)
    outward.wait()


def fluxes(flow, area):
    density = 1.0 + 0.2 * flow[0]
    velocity = [0.4 * flow[1 + i] for i in range(3)]
    normal_flux = velocity[0] * area[0] + velocity[1] * area[1] + velocity[2] * area[2]
    mass_flux = density * normal_flux
    return [mass_flux] + [flow[4] * area[i] + mass_flux * velocity[i] for i in range(3)]


def early_kernel(own_ref, offset_ref, flow_ref, area_ref, point_ref, field_ref, spread_ref, own_area_ref, own_point_ref, delay_ref):
    width = flow_ref.shape[2]
    for block in range(delay_ref.shape[0]):
        delay_ref[block] = offset_ref[own_ref[0], block]
    own_area_ref[...] = area_ref[...]
    own_point_ref[...] = point_ref[...]
    point = [(1.0 / SOUND_STEP) * point_ref[i : i + 1, :] for i in range(3)]
    reach = RADIUS * RADIUS + point[0] * point[0] + point[1] * point[1] + point[2] * point[2]
    turned = jnp.transpose(jnp.concatenate([2.0 * point[0], 2.0 * point[1], 2.0 * point[2], reach] * 2, axis=0))
    for cut in range(width // LANES):
        lanes = slice(cut * LANES, (cut + 1) * LANES)
        area = [area_ref[i : i + 1, lanes] for i in range(3)]
        for k, field in enumerate(fluxes([flow_ref[i, :, lanes] for i in range(5)], area)):
            field_ref[k, cut] = field
        for i in range(4):
            spread_ref[i, lanes, :] = jnp.broadcast_to(turned[lanes, i : i + 1], (LANES, LANES))


def terms_kernel(time_ref, early_ref, core_ref, chip_ref, area_ref, point_ref, terms_ref, field_ref, part_ref):
    steps = early_ref.shape[2]
    width = area_ref.shape[1]
    count = steps + ROWS
    even = time_ref[0] % 2 == 0
    low = jnp.where(even, chip_ref[...], core_ref[...])
    high = jnp.where(even, core_ref[:, :1, :], chip_ref[:, :1, :])
    for cut in range(width // LANES):
        lanes = slice(cut * LANES, (cut + 1) * LANES)
        area = [area_ref[i : i + 1, lanes] for i in range(3)]
        point = [(1.0 / SOUND_STEP) * point_ref[i : i + 1, lanes] for i in range(3)]
        field_ref[:, cut, ROWS + steps :, :] = jnp.zeros((4, ROWS, LANES), jnp.float32)
        field_ref[:, cut, ROWS : ROWS + steps, :] = early_ref[:, cut]
        for halo, start in ((low, ROWS - LAGS), (high, ROWS + steps)):
            for k, field in enumerate(fluxes(halo[:, :, lanes], area)):
                field_ref[k, cut, start : start + halo.shape[1], :] = field
        first = ROWS - LAGS + 1
        row = lax.broadcasted_iota(jnp.int32, (count, LANES), 0)
        keep = jnp.where(jnp.logical_or(row >= LAGS - 1, time_ref[0] != 0), 1.0, 0.0)
        rates = [
            (0.5 * keep)
            * (field_ref[k, cut, first + 1 : first + 1 + count, :] - field_ref[k, cut, first - 1 : first - 1 + count, :])
            for k in range(4)
        ]
        loads = [keep * field_ref[1 + i, cut, first : first + count, :] for i in range(3)]
        reach = RADIUS * RADIUS + point[0] * point[0] + point[1] * point[1] + point[2] * point[2]
        mass_rate = SOUND_STEP * rates[0]
        far = rates[1:] + [-(point[0] * rates[1] + point[1] * rates[2] + point[2] * rates[3])]
        near = [loads[i] - (2.0 * point[i]) * mass_rate for i in range(3)]
        near.append(reach * mass_rate - (point[0] * loads[0] + point[1] * loads[1] + point[2] * loads[2]))
        for family, parts in enumerate((far, near)):
            for comp, part in enumerate(parts):
                part_ref[cut, family * COMPS + comp] = part
        for family in range(2):
            for comp in range(COMPS):
                for lag in range(LAGS):
                    start = LAGS - 1 - lag
                    block = (cut * 2 + family) * LAGS + lag
                    terms_ref[block, comp * steps : (comp + 1) * steps, :] = part_ref[
                        cut, family * COMPS + comp, start : start + steps, :
                    ].astype(jnp.bfloat16)


def fill_weights(places, spread_ref, weights_ref, part):
    span = spread_ref.shape[1]
    for start in range(span * part // PARTS, span * (part + 1) // PARTS, CHUNK):
        rows = slice(start, start + CHUNK)
        spread = [spread_ref[i, rows, :] for i in range(4)]
        for group, place in enumerate(places):
            square = spread[3] - place[0] * spread[0] - place[1] * spread[1] - place[2] * spread[2]
            inverse = lax.rsqrt(square)
            behind = (1.0 + NEAREST) - square * inverse
            first = jnp.maximum(behind, 0.0)
            passed = first - behind
            last = jnp.maximum(passed - 1.0, 0.0)
            middle = jnp.minimum(passed, 1.0)
            tents = (first, (1.0 - middle) - first, middle - last, last)
            far = inverse * inverse
            near = far * inverse
            quarter = start // LANES
            for family, coeff in enumerate((far, near)):
                for index, tent in enumerate(tents):
                    base = ((quarter * 2 + family) * LAGS + index) * LANES + start % LANES
                    weights_ref[group, base : base + CHUNK, :] = (coeff * tent).astype(jnp.bfloat16)


def sine_cosine(angle):
    half = 0.5 * angle
    square = half * half
    sine = cosine = 0.0
    for k in range(7, -1, -1):
        cosine = cosine * square + (-1.0) ** k / math.factorial(2 * k)
        sine = sine * square + (-1.0) ** k / math.factorial(2 * k + 1)
    sine = half * sine
    return 2.0 * sine * cosine, 1.0 - 2.0 * sine * sine


def pair_kernel(angle_ref, terms_ref, spread_ref, sums_ref, angles_ref, places_ref, even_ref, odd_ref, held_ref, rest_ref):
    groups, steps, lanes = sums_ref.shape
    for group in range(groups):
        for i in range(2):
            angles_ref[i, group : group + 1, :] = angle_ref[group, i : i + 1, :]
    sine, cosine = sine_cosine(angles_ref[0])
    rise, flat = sine_cosine(angles_ref[1])
    places_ref[0] = RADIUS * (cosine * flat)
    places_ref[1] = RADIUS * (sine * flat)
    places_ref[2] = RADIUS * rise
    pair = even_ref.shape[0]
    turns = groups // pair
    blocks = terms_ref.shape[0]

    def places_of(turn):
        return [[places_ref[i, pl.ds(turn * pair + j, 1), :] for i in range(3)] for j in range(pair)]

    def multiply(weights_ref, make):
        total = None
        for part in range(PARTS):
            span = range(blocks * part // PARTS, blocks * (part + 1) // PARTS)
            terms = jnp.concatenate([terms_ref[k] for k in span], axis=1)
            rows = slice(span[0] * LANES, (span[-1] + 1) * LANES)
            weights = jnp.concatenate([weights_ref[j, rows, :] for j in range(pair)], axis=1)
            piece = jnp.dot(terms, weights, preferred_element_type=jnp.float32)
            total = piece if total is None else total + piece
            make(part)
        return total

    def finish(turn, total_ref):
        for j, place in enumerate(places_of(turn)):
            mine = total_ref[:, j * lanes : (j + 1) * lanes]
            result = mine[3 * steps :]
            for i in range(3):
                result = result + place[i] * mine[i * steps : (i + 1) * steps]
            sums_ref[turn * pair + j] = (SCALE * result).astype(sums_ref.dtype)

    for part in range(PARTS):
        fill_weights(places_of(0), spread_ref, even_ref, part)

    def body(step, carry):
        even = 2 * step
        odd = 2 * step + 1

        @pl.when(step >= 0)
        def _():
            finish(jnp.maximum(even - 1, 0), rest_ref)
            places = places_of(odd)
            held_ref[...] = multiply(even_ref, lambda part: fill_weights(places, spread_ref, odd_ref, part))

        @pl.when(odd < turns - 1)
        def _():
            finish(even, held_ref)
            places = places_of(odd + 1)
            rest_ref[...] = multiply(odd_ref, lambda part: fill_weights(places, spread_ref, even_ref, part))

        return carry

    lax.fori_loop(0, turns // 2, body, 0)
    finish(turns - 2, held_ref)
    rest_ref[...] = multiply(odd_ref, lambda part: None)
    finish(turns - 1, rest_ref)


def place_kernel(delay_ref, sums_ref, out_ref, later_ref, canvas_ref):
    groups, steps, _ = sums_ref.shape
    canvas_ref[...] = jnp.zeros_like(canvas_ref)
    for block in range(groups):
        span = pl.ds(delay_ref[block], steps)
        canvas_ref[span, :] = canvas_ref[span, :] + sums_ref[block].astype(jnp.float32)
    out_ref[...] = canvas_ref[:steps]
    later_ref[...] = canvas_ref[steps : 2 * steps]


VMEM = pl.BlockSpec(memory_space=pltpu.VMEM)
SMEM = pl.BlockSpec(memory_space=pltpu.SMEM)
HBM = pl.BlockSpec(memory_space=pltpu.HBM)


def near_core(array):
    return pltpu.with_memory_space_constraint(array, pltpu.VMEM)


def in_hbm(array):
    return pltpu.with_memory_space_constraint(array, pltpu.HBM)


def local(flow, point_pos, area_vec, observer_angles, band_offset):
    steps = flow.shape[1]
    width = flow.shape[2]
    groups = lax.axis_size("obs")
    lanes = observer_angles.shape[1]
    times = lax.axis_size("tm")
    time = lax.axis_index("tm").astype(jnp.int32).reshape(1)
    wide, to_core, to_chip = pl.pallas_call(
        prep_kernel,
        out_shape=(
            jax.ShapeDtypeStruct((groups, 2, lanes), jnp.float32),
            pltpu.VMEM((5, LAGS, width), jnp.float32),
            pltpu.VMEM((5, LAGS, width), jnp.float32),
        ),
        in_specs=[SMEM, HBM, HBM],
        out_specs=(HBM, VMEM, VMEM),
        scratch_shapes=[
            pltpu.VMEM((2, 5, ROWS, width), jnp.float32),
            pltpu.VMEM((2, lanes), jnp.float32),
            pltpu.VMEM((groups, 2, lanes), jnp.float32),
            pltpu.SemaphoreType.DMA((4,)),
        ],
        compiler_params=pltpu.CompilerParams(vmem_limit_bytes=8 << 20),
        name="prep",
    )(time, in_hbm(flow), in_hbm(observer_angles))
    angles = lax.all_to_all(wide, "obs", 0, 0, tiled=True)
    from_core = lax.ppermute(to_core, "tm", [(i, i ^ 1) for i in range(times)])
    swaps = [(i, i + 1) for i in range(1, times - 1, 2)]
    from_chip = lax.ppermute(to_chip, "tm", swaps + [(j, i) for i, j in swaps])
    own = lax.axis_index("obs").astype(jnp.int32).reshape(1)
    depth = 2 * LAGS * width
    cuts = width // LANES
    early, spread, own_area, own_point, delays = pl.pallas_call(
        early_kernel,
        out_shape=(
            pltpu.VMEM((4, cuts, steps, LANES), jnp.float32),
            pltpu.VMEM((4, width, LANES), jnp.float32),
            pltpu.VMEM(area_vec.shape, jnp.float32),
            pltpu.VMEM(point_pos.shape, jnp.float32),
            pltpu.SMEM((groups,), jnp.int32),
        ),
        in_specs=[SMEM] * 2 + [VMEM] * 3,
        out_specs=(VMEM,) * 4 + (SMEM,),
        compiler_params=pltpu.CompilerParams(vmem_limit_bytes=16 << 20),
        name="early",
    )(own, in_hbm(band_offset), in_hbm(flow), in_hbm(area_vec), in_hbm(point_pos))
    terms = pl.pallas_call(
        terms_kernel,
        out_shape=pltpu.VMEM((depth // LANES, COMPS * steps, LANES), jnp.bfloat16),
        in_specs=[SMEM] + [VMEM] * 5,
        out_specs=VMEM,
        scratch_shapes=[
            pltpu.VMEM((4, cuts, steps + 2 * ROWS, LANES), jnp.float32),
            pltpu.VMEM((cuts, 2 * COMPS, steps + ROWS, LANES), jnp.float32),
        ],
        compiler_params=pltpu.CompilerParams(vmem_limit_bytes=16 << 20),
        name="terms",
    )(time, *map(near_core, (early, from_core, from_chip, own_area, own_point)))
    pair = 2
    sums = pl.pallas_call(
        pair_kernel,
        out_shape=pltpu.VMEM((groups, steps, lanes), jnp.bfloat16),
        in_specs=[VMEM] * 3,
        out_specs=VMEM,
        scratch_shapes=[
            pltpu.VMEM((2, groups, lanes), jnp.float32),
            pltpu.VMEM((3, groups, lanes), jnp.float32),
            pltpu.VMEM((pair, depth, lanes), jnp.bfloat16),
            pltpu.VMEM((pair, depth, lanes), jnp.bfloat16),
            pltpu.VMEM((COMPS * steps, pair * lanes), jnp.float32),
            pltpu.VMEM((COMPS * steps, pair * lanes), jnp.float32),
        ],
        compiler_params=pltpu.CompilerParams(vmem_limit_bytes=24 << 20),
        name="pairs",
    )(near_core(angles), near_core(terms), near_core(spread))
    sums = lax.all_to_all(sums, "obs", 0, 0, tiled=True)
    out, later = pl.pallas_call(
        place_kernel,
        out_shape=(pltpu.VMEM((steps, lanes), jnp.float32),) * 2,
        in_specs=[SMEM, VMEM],
        out_specs=(VMEM, VMEM),
        scratch_shapes=[pltpu.VMEM((2 * steps, lanes), jnp.float32)],
        compiler_params=pltpu.CompilerParams(vmem_limit_bytes=8 << 20),
        name="place",
    )(pltpu.with_memory_space_constraint(delays, pltpu.SMEM), near_core(sums))
    carried = lax.ppermute(later, "tm", [(i, i + 1) for i in range(times - 1)])
    return out + carried


def solution(mesh):
    in_specs = (P(None, "tm", "obs"), P(None, "obs"), P(None, "obs"), P(None, "obs"), P())
    out_specs = P("tm", "obs")
    return jax.shard_map(local, mesh=mesh, in_specs=in_specs, out_specs=out_specs, check_vma=False)
```

```python
import math

import jax
import jax.numpy as jnp
from jax import lax
from jax.experimental import pallas as pl
from jax.experimental.pallas import tpu as pltpu
from jax.sharding import PartitionSpec as P


LAGS = 4
NEAR_RANGE = 3.25
SOUND_STEP = 1.17
RADIUS = 5.0 / SOUND_STEP
NEAREST = NEAR_RANGE / SOUND_STEP
SCALE = 1.0 / (4.0 * math.pi * SOUND_STEP * SOUND_STEP)
COMPS = 4
ROWS = 8
LANES = 128
CHUNK = 16
PARTS = 16


def prep_kernel(time_ref, flow_ref, angle_ref, wide_ref, core_ref, chip_ref, edges_ref, held_ref, spread_ref, sem):
    steps = flow_ref.shape[1]
    inward = pltpu.make_async_copy(angle_ref, held_ref, sem.at[2])
    inward.start()
    copies = [
        pltpu.make_async_copy(flow_ref.at[:, pl.ds(start, ROWS), :], edges_ref.at[side], sem.at[side])
        for side, start in enumerate((steps - ROWS, 0))
    ]
    for copy in copies:
        copy.start()
    inward.wait()
    for group in range(spread_ref.shape[0]):
        spread_ref[group] = held_ref[...]
    outward = pltpu.make_async_copy(spread_ref, wide_ref, sem.at[3])
    outward.start()
    for copy in copies:
        copy.wait()
    even = time_ref[0] % 2 == 0
    last = edges_ref[0, :, ROWS - LAGS :, :]
    first = edges_ref[1, :, :LAGS, :]
    core_ref[...] = jnp.where(even, last, first)
    chip_ref[...] = jnp.where(even, first, last)
    outward.wait()


def fluxes(flow, area):
    density = 1.0 + 0.2 * flow[0]
    velocity = [0.4 * flow[1 + i] for i in range(3)]
    normal_flux = velocity[0] * area[0] + velocity[1] * area[1] + velocity[2] * area[2]
    mass_flux = density * normal_flux
    return [mass_flux] + [flow[4] * area[i] + mass_flux * velocity[i] for i in range(3)]


def early_kernel(
    own_ref, offset_ref, flow_ref, area_ref, point_ref, field_ref, spread_ref, own_area_ref, own_point_ref, delay_ref,
    held_ref, table_ref, sem,
):
    width = flow_ref.shape[2]
    routes = ((point_ref, own_point_ref), (area_ref, own_area_ref), (flow_ref, held_ref), (offset_ref, table_ref))
    copies = [pltpu.make_async_copy(source, target, sem.at[i]) for i, (source, target) in enumerate(routes)]
    for copy in copies:
        copy.start()
    copies[0].wait()
    point = [(1.0 / SOUND_STEP) * own_point_ref[i : i + 1, :] for i in range(3)]
    reach = RADIUS * RADIUS + point[0] * point[0] + point[1] * point[1] + point[2] * point[2]
    turned = jnp.transpose(jnp.concatenate([2.0 * point[0], 2.0 * point[1], 2.0 * point[2], reach] * 2, axis=0))
    for i in range(4):
        spread_ref[i] = jnp.broadcast_to(turned[:, i : i + 1], spread_ref.shape[1:])
    copies[1].wait()
    copies[2].wait()
    for cut in range(width // LANES):
        lanes = slice(cut * LANES, (cut + 1) * LANES)
        area = [own_area_ref[i : i + 1, lanes] for i in range(3)]
        for k, field in enumerate(fluxes([held_ref[i, :, lanes] for i in range(5)], area)):
            field_ref[k, cut] = field
    copies[3].wait()
    for block in range(delay_ref.shape[0]):
        delay_ref[block] = table_ref[own_ref[0], block]


def terms_kernel(time_ref, early_ref, core_ref, chip_ref, area_ref, point_ref, terms_ref, field_ref, part_ref):
    steps = early_ref.shape[2]
    width = area_ref.shape[1]
    count = steps + ROWS
    even = time_ref[0] % 2 == 0
    low = jnp.where(even, chip_ref[...], core_ref[...])
    high = jnp.where(even, core_ref[:, :1, :], chip_ref[:, :1, :])
    for cut in range(width // LANES):
        lanes = slice(cut * LANES, (cut + 1) * LANES)
        area = [area_ref[i : i + 1, lanes] for i in range(3)]
        point = [(1.0 / SOUND_STEP) * point_ref[i : i + 1, lanes] for i in range(3)]
        field_ref[:, cut, ROWS + steps :, :] = jnp.zeros((4, ROWS, LANES), jnp.float32)
        field_ref[:, cut, ROWS : ROWS + steps, :] = early_ref[:, cut]
        for halo, start in ((low, ROWS - LAGS), (high, ROWS + steps)):
            for k, field in enumerate(fluxes(halo[:, :, lanes], area)):
                field_ref[k, cut, start : start + halo.shape[1], :] = field
        first = ROWS - LAGS + 1
        row = lax.broadcasted_iota(jnp.int32, (count, LANES), 0)
        keep = jnp.where(jnp.logical_or(row >= LAGS - 1, time_ref[0] != 0), 1.0, 0.0)
        rates = [
            (0.5 * keep)
            * (field_ref[k, cut, first + 1 : first + 1 + count, :] - field_ref[k, cut, first - 1 : first - 1 + count, :])
            for k in range(4)
        ]
        loads = [keep * field_ref[1 + i, cut, first : first + count, :] for i in range(3)]
        reach = RADIUS * RADIUS + point[0] * point[0] + point[1] * point[1] + point[2] * point[2]
        mass_rate = SOUND_STEP * rates[0]
        far = rates[1:] + [-(point[0] * rates[1] + point[1] * rates[2] + point[2] * rates[3])]
        near = [loads[i] - (2.0 * point[i]) * mass_rate for i in range(3)]
        near.append(reach * mass_rate - (point[0] * loads[0] + point[1] * loads[1] + point[2] * loads[2]))
        for family, parts in enumerate((far, near)):
            for comp, part in enumerate(parts):
                part_ref[cut, family * COMPS + comp] = part
        for family in range(2):
            for comp in range(COMPS):
                for lag in range(LAGS):
                    start = LAGS - 1 - lag
                    block = (cut * 2 + family) * LAGS + lag
                    terms_ref[block, comp * steps : (comp + 1) * steps, :] = part_ref[
                        cut, family * COMPS + comp, start : start + steps, :
                    ].astype(jnp.bfloat16)


def fill_weights(places, spread_ref, weights_ref, part):
    span = spread_ref.shape[1]
    for start in range(span * part // PARTS, span * (part + 1) // PARTS, CHUNK):
        rows = slice(start, start + CHUNK)
        spread = [spread_ref[i, rows, :] for i in range(4)]
        for group, place in enumerate(places):
            square = spread[3] - place[0] * spread[0] - place[1] * spread[1] - place[2] * spread[2]
            inverse = lax.rsqrt(square)
            behind = (1.0 + NEAREST) - square * inverse
            first = jnp.maximum(behind, 0.0)
            passed = first - behind
            last = jnp.maximum(passed - 1.0, 0.0)
            middle = jnp.minimum(passed, 1.0)
            tents = (first, (1.0 - middle) - first, middle - last, last)
            far = inverse * inverse
            near = far * inverse
            quarter = start // LANES
            for family, coeff in enumerate((far, near)):
                for index, tent in enumerate(tents):
                    base = ((quarter * 2 + family) * LAGS + index) * LANES + start % LANES
                    weights_ref[group, base : base + CHUNK, :] = (coeff * tent).astype(jnp.bfloat16)


def sine_cosine(angle):
    half = 0.5 * angle
    square = half * half
    sine = cosine = 0.0
    for k in range(7, -1, -1):
        cosine = cosine * square + (-1.0) ** k / math.factorial(2 * k)
        sine = sine * square + (-1.0) ** k / math.factorial(2 * k + 1)
    sine = half * sine
    return 2.0 * sine * cosine, 1.0 - 2.0 * sine * sine


def pair_kernel(angle_ref, terms_ref, spread_ref, sums_ref, angles_ref, places_ref, even_ref, odd_ref, held_ref, rest_ref):
    groups, steps, lanes = sums_ref.shape
    for group in range(groups):
        for i in range(2):
            angles_ref[i, group : group + 1, :] = angle_ref[group, i : i + 1, :]
    sine, cosine = sine_cosine(angles_ref[0])
    rise, flat = sine_cosine(angles_ref[1])
    places_ref[0] = RADIUS * (cosine * flat)
    places_ref[1] = RADIUS * (sine * flat)
    places_ref[2] = RADIUS * rise
    pair = even_ref.shape[0]
    turns = groups // pair
    blocks = terms_ref.shape[0]

    def places_of(turn):
        return [[places_ref[i, pl.ds(turn * pair + j, 1), :] for i in range(3)] for j in range(pair)]

    def multiply(weights_ref, make):
        total = None
        for part in range(PARTS):
            span = range(blocks * part // PARTS, blocks * (part + 1) // PARTS)
            terms = jnp.concatenate([terms_ref[k] for k in span], axis=1)
            rows = slice(span[0] * LANES, (span[-1] + 1) * LANES)
            weights = jnp.concatenate([weights_ref[j, rows, :] for j in range(pair)], axis=1)
            piece = jnp.dot(terms, weights, preferred_element_type=jnp.float32)
            total = piece if total is None else total + piece
            make(part)
        return total

    def finish(turn, total_ref):
        for j, place in enumerate(places_of(turn)):
            mine = total_ref[:, j * lanes : (j + 1) * lanes]
            result = mine[3 * steps :]
            for i in range(3):
                result = result + place[i] * mine[i * steps : (i + 1) * steps]
            sums_ref[turn * pair + j] = (SCALE * result).astype(sums_ref.dtype)

    for part in range(PARTS):
        fill_weights(places_of(0), spread_ref, even_ref, part)

    def body(step, carry):
        even = 2 * step
        odd = 2 * step + 1

        @pl.when(step >= 0)
        def _():
            finish(jnp.maximum(even - 1, 0), rest_ref)
            places = places_of(odd)
            held_ref[...] = multiply(even_ref, lambda part: fill_weights(places, spread_ref, odd_ref, part))

        @pl.when(odd < turns - 1)
        def _():
            finish(even, held_ref)
            places = places_of(odd + 1)
            rest_ref[...] = multiply(odd_ref, lambda part: fill_weights(places, spread_ref, even_ref, part))

        return carry

    lax.fori_loop(0, turns // 2, body, 0)
    rest_ref[...] = multiply(odd_ref, lambda part: finish(turns - 2, held_ref) if part == 2 else None)
    finish(turns - 1, rest_ref)


def place_kernel(delay_ref, sums_ref, out_ref, later_ref, canvas_ref):
    groups, steps, _ = sums_ref.shape
    canvas_ref[...] = jnp.zeros_like(canvas_ref)
    for block in range(groups):
        span = pl.ds(delay_ref[block], steps)
        canvas_ref[span, :] = canvas_ref[span, :] + sums_ref[block].astype(jnp.float32)
    out_ref[...] = canvas_ref[:steps]
    later_ref[...] = canvas_ref[steps : 2 * steps]


VMEM = pl.BlockSpec(memory_space=pltpu.VMEM)
SMEM = pl.BlockSpec(memory_space=pltpu.SMEM)
HBM = pl.BlockSpec(memory_space=pltpu.HBM)


def near_core(array):
    return pltpu.with_memory_space_constraint(array, pltpu.VMEM)


def in_hbm(array):
    return pltpu.with_memory_space_constraint(array, pltpu.HBM)


def local(flow, point_pos, area_vec, observer_angles, band_offset):
    steps = flow.shape[1]
    width = flow.shape[2]
    groups = lax.axis_size("obs")
    lanes = observer_angles.shape[1]
    times = lax.axis_size("tm")
    time = lax.axis_index("tm").astype(jnp.int32).reshape(1)
    wide, to_core, to_chip = pl.pallas_call(
        prep_kernel,
        out_shape=(
            jax.ShapeDtypeStruct((groups, 2, lanes), jnp.float32),
            pltpu.VMEM((5, LAGS, width), jnp.float32),
            pltpu.VMEM((5, LAGS, width), jnp.float32),
        ),
        in_specs=[SMEM, HBM, HBM],
        out_specs=(HBM, VMEM, VMEM),
        scratch_shapes=[
            pltpu.VMEM((2, 5, ROWS, width), jnp.float32),
            pltpu.VMEM((2, lanes), jnp.float32),
            pltpu.VMEM((groups, 2, lanes), jnp.float32),
            pltpu.SemaphoreType.DMA((4,)),
        ],
        compiler_params=pltpu.CompilerParams(vmem_limit_bytes=8 << 20),
        name="prep",
    )(time, in_hbm(flow), in_hbm(observer_angles))
    angles = lax.all_to_all(wide, "obs", 0, 0, tiled=True)
    from_core = lax.ppermute(to_core, "tm", [(i, i ^ 1) for i in range(times)])
    swaps = [(i, i + 1) for i in range(1, times - 1, 2)]
    from_chip = lax.ppermute(to_chip, "tm", swaps + [(j, i) for i, j in swaps])
    own = lax.axis_index("obs").astype(jnp.int32).reshape(1)
    depth = 2 * LAGS * width
    cuts = width // LANES
    early, spread, own_area, own_point, delays = pl.pallas_call(
        early_kernel,
        out_shape=(
            pltpu.VMEM((4, cuts, steps, LANES), jnp.float32),
            pltpu.VMEM((4, width, LANES), jnp.float32),
            pltpu.VMEM(area_vec.shape, jnp.float32),
            pltpu.VMEM(point_pos.shape, jnp.float32),
            pltpu.SMEM((groups,), jnp.int32),
        ),
        in_specs=[SMEM] + [HBM] * 4,
        out_specs=(VMEM,) * 4 + (SMEM,),
        scratch_shapes=[
            pltpu.VMEM(flow.shape, jnp.float32),
            pltpu.SMEM(band_offset.shape, jnp.int32),
            pltpu.SemaphoreType.DMA((4,)),
        ],
        compiler_params=pltpu.CompilerParams(vmem_limit_bytes=16 << 20),
        name="early",
    )(own, in_hbm(band_offset), in_hbm(flow), in_hbm(area_vec), in_hbm(point_pos))
    terms = pl.pallas_call(
        terms_kernel,
        out_shape=pltpu.VMEM((depth // LANES, COMPS * steps, LANES), jnp.bfloat16),
        in_specs=[SMEM] + [VMEM] * 5,
        out_specs=VMEM,
        scratch_shapes=[
            pltpu.VMEM((4, cuts, steps + 2 * ROWS, LANES), jnp.float32),
            pltpu.VMEM((cuts, 2 * COMPS, steps + ROWS, LANES), jnp.float32),
        ],
        compiler_params=pltpu.CompilerParams(vmem_limit_bytes=16 << 20),
        name="terms",
    )(time, *map(near_core, (early, from_core, from_chip, own_area, own_point)))
    pair = 2
    sums = pl.pallas_call(
        pair_kernel,
        out_shape=pltpu.VMEM((groups, steps, lanes), jnp.bfloat16),
        in_specs=[VMEM] * 3,
        out_specs=VMEM,
        scratch_shapes=[
            pltpu.VMEM((2, groups, lanes), jnp.float32),
            pltpu.VMEM((3, groups, lanes), jnp.float32),
            pltpu.VMEM((pair, depth, lanes), jnp.bfloat16),
            pltpu.VMEM((pair, depth, lanes), jnp.bfloat16),
            pltpu.VMEM((COMPS * steps, pair * lanes), jnp.float32),
            pltpu.VMEM((COMPS * steps, pair * lanes), jnp.float32),
        ],
        compiler_params=pltpu.CompilerParams(vmem_limit_bytes=24 << 20),
        name="pairs",
    )(near_core(angles), near_core(terms), near_core(spread))
    sums = lax.all_to_all(sums, "obs", 0, 0, tiled=True)
    out, later = pl.pallas_call(
        place_kernel,
        out_shape=(pltpu.VMEM((steps, lanes), jnp.float32),) * 2,
        in_specs=[SMEM, VMEM],
        out_specs=(VMEM, VMEM),
        scratch_shapes=[pltpu.VMEM((2 * steps, lanes), jnp.float32)],
        compiler_params=pltpu.CompilerParams(vmem_limit_bytes=8 << 20),
        name="place",
    )(pltpu.with_memory_space_constraint(delays, pltpu.SMEM), near_core(sums))
    carried = lax.ppermute(later, "tm", [(i, i + 1) for i in range(times - 1)])
    return out + carried


def solution(mesh):
    in_specs = (P(None, "tm", "obs"), P(None, "obs"), P(None, "obs"), P(None, "obs"), P())
    out_specs = P("tm", "obs")
    return jax.shard_map(local, mesh=mesh, in_specs=in_specs, out_specs=out_specs, check_vma=False)
```
